256 devices in a mesh: coord: 64 (over y, x_lo, z), ka: 4 (over x_hi, core).
Axes of the slice: x: 4 (x_hi: 2, x_lo: 2; x = x_hi * 2 + x_lo), y: 4, z: 8, core: 2. Of those that a mesh axis runs over, the one named last changes fastest.
Arguments:
- states: float32 [4, 512, 512, 128], P('ka', 'coord'), may hold values from -6 to 6
- potential: float32 [512, 512, 128], P('coord'), may hold values from 0 to 3
- rotation_factor: float32 [512, 512], P('coord'), may hold values from 0.05 to 0.4
- basis_first: float32 [512, 512], replicated, may hold values from -0.25 to 0.25
- basis_second: float32 [512, 512], replicated, may hold values from -0.25 to 0.25
- basis_third: float32 [128, 128], replicated, may hold values from -0.5 to 0.5
- levels_first: float32 [512], replicated, may hold values from 0 to 2
- levels_second: float32 [512], replicated, may hold values from 0 to 2
- levels_third: float32 [128], replicated, may hold values from 0 to 2
- kinetic_first: float32 [512, 512], replicated, as said below
- kinetic_second: float32 [512, 512], replicated, as said below
- kinetic_third: float32 [128, 128], replicated, as said below
- coriolis_matrix: float32 [128, 128], replicated, may hold values from -0.5 to 0.5
Outputs:
- correction: float32 [4, 512, 512, 128], P('ka', 'coord')
- residual: float32 [4, 512, 512, 128], P('ka', 'coord')
The draws below stay inside these ranges and needn't reach their ends.
Inputs may be any that keep to these rules, and one draw needn't show every extreme that they name: `kinetic_first`: symmetric. `kinetic_second`: symmetric. `kinetic_third`: symmetric.
All inputs are finite; a program needn't handle non-finite values.
Results may differ from the reference program's by a relative error of at most 0.000052.
Values sent between devices are 32-bit elements; how exact they have to be, the bound alone decides.
A program may use at most 128 MiB of HBM per device.

```python
import math
import jax
import jax.numpy as jnp
from jax import lax

N1 = 512
N2 = 512
N3 = 128
K_BLOCKS = 4


def symmetric_draw(key, salt, order):
    local = jax.random.fold_in(key, salt)
    entries = jax.random.uniform(local, (order, order), jnp.float32, -1.0, 1.0)
    return (entries + entries.T) * (0.5 / math.sqrt(order)) + jnp.eye(order, dtype=jnp.float32)


def draw_kinetic_first(key, part):
    return symmetric_draw(key, 11, N1)


def draw_kinetic_second(key, part):
    return symmetric_draw(key, 23, N2)


def draw_kinetic_third(key, part):
    return symmetric_draw(key, 37, N3)


def steps_of(stream_key, shape, shards, least, top_value):
    gain = 1.0
    for position, blocks in shards:
        heights = jax.random.uniform(jax.random.fold_in(jax.random.fold_in(stream_key, 6), position), (blocks,), jnp.float32, least / len(shards), top_value / len(shards))
        gain = gain * jnp.repeat(jnp.exp(heights), shape[position] // blocks).reshape((-1,) + (1,) * (len(shape) - 1 - position))
    return gain


def bell_draw(rng, shape, scale, most, pieces=(), kind=jnp.bfloat16):
    values = scale * jax.random.normal(rng, shape, jnp.float32)
    if pieces:
        values = values * steps_of(rng, shape, pieces, -0.22, 0.18)
    return jnp.clip(values, -most, most).astype(kind)


def setup_inputs(seed: int = 0) -> dict:
    arg_keys = jax.random.split(jax.random.key(seed), 14)
    states = bell_draw(arg_keys[0], (K_BLOCKS, N1, N2, N3), 1.0, 6.0, ((0, 4), (1, 64)), jnp.float32)
    potential = jnp.clip(3.0 * jax.random.uniform(arg_keys[1], (N1, N2, N3), jnp.float32) ** steps_of(arg_keys[1], (N1, N2, N3), ((0, 64),), -0.2, 0.2), 0.0, 3.0)
    rotation_factor = jnp.clip(0.05 + 0.35 * jax.random.uniform(arg_keys[2], (N1, N2), jnp.float32) ** steps_of(arg_keys[2], (N1, N2), ((0, 64),), -0.2, 0.2), 0.05, 0.4)
    basis_first = bell_draw(arg_keys[3], (N1, N1), N1 ** -0.5, 0.25, (), jnp.float32)
    basis_second = bell_draw(arg_keys[4], (N2, N2), N2 ** -0.5, 0.25, (), jnp.float32)
    basis_third = bell_draw(arg_keys[5], (N3, N3), N3 ** -0.5, 0.5, (), jnp.float32)
    levels_first = jnp.clip(jax.random.uniform(arg_keys[6], (N1,), jnp.float32, 0.0, 2.0), 0.0, 2.0)
    levels_second = jnp.clip(jax.random.uniform(arg_keys[7], (N2,), jnp.float32, 0.0, 2.0), 0.0, 2.0)
    levels_third = jnp.clip(jax.random.uniform(arg_keys[8], (N3,), jnp.float32, 0.0, 2.0), 0.0, 2.0)
    kinetic_first = draw_kinetic_first(jax.random.fold_in(arg_keys[13], 71), 0)
    kinetic_second = draw_kinetic_second(jax.random.fold_in(arg_keys[13], 71), 0)
    kinetic_third = draw_kinetic_third(jax.random.fold_in(arg_keys[13], 71), 0)
    coriolis_matrix = bell_draw(arg_keys[12], (N3, N3), N3 ** -0.5, 0.5, (), jnp.float32)
    return dict(states=states, potential=potential, rotation_factor=rotation_factor, basis_first=basis_first, basis_second=basis_second, basis_third=basis_third, levels_first=levels_first, levels_second=levels_second, levels_third=levels_third, kinetic_first=kinetic_first, kinetic_second=kinetic_second, kinetic_third=kinetic_third, coriolis_matrix=coriolis_matrix)


highest = lax.Precision.HIGHEST
shift_energy = 2.5
damping = 0.5

def settle(block, basis_first, basis_second, basis_third, filt):
    coeff = jnp.einsum('ijk,kc->ijc', block, basis_third, precision=highest)
    coeff = jnp.einsum('ijc,jb->ibc', coeff, basis_second, precision=highest)
    coeff = jnp.einsum('ibc,ia->abc', coeff, basis_first, precision=highest)
    coeff = coeff * filt
    back = jnp.einsum('ia,abc->ibc', basis_first, coeff, precision=highest)
    back = jnp.einsum('jb,ibc->ijc', basis_second, back, precision=highest)
    return jnp.einsum('kc,ijc->ijk', basis_third, back, precision=highest)

def reference(states, potential, rotation_factor, basis_first, basis_second, basis_third, levels_first, levels_second, levels_third, kinetic_first, kinetic_second, kinetic_third, coriolis_matrix):
    level = levels_first[:, None, None] + levels_second[None, :, None] + levels_third[None, None, :] - shift_energy
    filt = level / (level * level + damping * damping)

    def precondition(block):
        return settle(block, basis_first, basis_second, basis_third, filt)
    correction = lax.map(precondition, states)
    zeros = jnp.zeros_like(correction[:1])
    upper = jnp.concatenate([correction[1:], zeros], axis=0)
    lower = jnp.concatenate([zeros, correction[:-1]], axis=0)
    kvalues = jnp.arange(K_BLOCKS).astype(jnp.float32)
    square_top = (K_BLOCKS - 1) * K_BLOCKS
    factor = rotation_factor[:, :, None]

    def apply_block(items):
        source, solved, above, below, kval = items
        kinetic = jnp.einsum('im,mjk->ijk', kinetic_first, solved, precision=highest)
        kinetic = kinetic + jnp.einsum('jm,imk->ijk', kinetic_second, solved, precision=highest)
        kinetic = kinetic + jnp.einsum('km,ijm->ijk', kinetic_third, solved, precision=highest)
        coupled_up = jnp.sqrt(square_top - kval * (kval + 1.0))
        coupled_down = jnp.sqrt(square_top - (kval - 1.0) * kval)
        from_upper = jnp.einsum('km,ijm->ijk', coriolis_matrix, above, precision=highest)
        from_lower = jnp.einsum('mk,ijm->ijk', coriolis_matrix, below, precision=highest)
        coupling = factor * (coupled_up * from_upper + coupled_down * from_lower)
        applied = kinetic + (potential + kval * kval * factor) * solved + coupling
        return source - (applied - shift_energy * solved)
    residual = lax.map(apply_block, (states, correction, upper, lower, kvalues))
    return (correction, residual)
```

```python
import functools
import math

import jax
import jax.numpy as jnp
from jax import lax
from jax.experimental import pallas as pl
from jax.experimental.pallas import tpu as pltpu
from jax.sharding import PartitionSpec as P

MESH = pl.DeviceIdType.MESH
f32 = jnp.float32
bf16 = jnp.bfloat16
shift_energy = 2.5
damping = 0.5

PEERS = 64
BLOCKS = 4
GROUPS = 4
N1 = 512
N2 = 512
N3 = 128
ROWS = N1 // PEERS
PAIRS = ROWS // 2
SPAN = N2 // GROUPS
OWN = SPAN // PEERS


def split(value):
    high = value.astype(bf16)
    return high, (value - high.astype(f32)).astype(bf16)


def dot(left, right):
    return jnp.dot(left, right, preferred_element_type=f32)


def put_weight(ref, value, offset=0):
    high, low = split(value)
    width = value.shape[1]
    for place, part in enumerate((high, low, high)):
        ref[pl.ds(offset, value.shape[0]), pl.ds(place * width, width)] = part


def put_data(ref, value, lane):
    high, low = split(value)
    height, width = value.shape
    for place, part in enumerate((high, high, low)):
        ref[pl.ds(place * height, height), pl.ds(lane, width)] = part


def spread(row, height=N3):
    return jnp.broadcast_to(row, (height, row.shape[1])).T


def kernel(
    states,
    potential,
    rotation,
    first,
    second,
    third,
    levels_first,
    levels_second,
    levels_third,
    kin_first,
    kin_second,
    kin_third,
    coriolis,
    solved_out,
    residual_out,
    src,
    pot,
    rot,
    b1,
    b2,
    k1,
    k2,
    b3,
    k3,
    cor,
    w_b2t,
    w_b1t,
    w_b1,
    w_k1,
    w_b2,
    w_kb,
    u1,
    u2,
    cols,
    xs,
    ys,
    xr,
    yr,
    above,
    below,
    data,
    lx,
    ly,
    t1,
    t2,
    tv,
    w_a,
    w_al,
    w_b,
    w_v,
    w_vl,
    acc_p,
    acc_v,
    diag,
    wide,
    lev1,
    load_sem,
    out_sem,
    fwd_send,
    fwd_recv,
    x_send,
    x_recv,
    y_send,
    y_recv,
    up_send,
    up_recv,
    down_send,
    down_recv,
):
    me = lax.axis_index("coord")
    ka = lax.axis_index("ka")
    my_y, my_x, my_z = me // 16, lax.rem(me // 8, 2), lax.rem(me, 8)

    def peer(step):
        dy, dx, dz = step // 16, lax.rem(step // 8, 2), lax.rem(step, 8)
        return lax.rem(my_y + dy, 4) * 16 + lax.rem(my_x + dx, 2) * 8 + lax.rem(my_z + dz, 8)

    def each_peer(body):
        def step(s, carry):
            body(peer(s))
            return carry

        lax.fori_loop(1, PEERS, step, 0)

    barrier = pltpu.get_barrier_semaphore()
    each_peer(
        lambda p: pl.semaphore_signal(barrier, inc=1, device_id=(p, ka), device_id_type=MESH)
    )

    @pl.when(ka > 0)
    def _():
        pl.semaphore_signal(barrier, inc=1, device_id=(me, ka - 1), device_id_type=MESH)

    @pl.when(ka < BLOCKS - 1)
    def _():
        pl.semaphore_signal(barrier, inc=1, device_id=(me, ka + 1), device_id_type=MESH)

    loads = []
    for index, (source, target) in enumerate(
        (
            (third, b3),
            (states.at[0], src),
            (second, b2),
            (first, b1),
            (kin_first, k1),
            (kin_third, k3),
            (coriolis, cor),
            (kin_second, k2),
            (potential, pot),
            (rotation, rot),
        )
    ):
        copy = pltpu.make_async_copy(source, target, load_sem.at[index])
        copy.start()
        loads.append(copy)

    loads[0].wait()
    high, low = split(b3[...])
    w_b[0:N3, 0:N3] = high
    w_b[N3 : 2 * N3, 0:N3] = high
    w_b[0:N3, N3 : 2 * N3] = low
    w_b[N3 : 2 * N3, N3 : 2 * N3] = jnp.zeros((N3, N3), bf16)
    loads[1].wait()

    @pl.loop(0, ROWS)
    def _(i):
        high, low = split(src[i])
        lx[0:N2, 0:N3] = high
        lx[0:N2, N3 : 2 * N3] = low
        both = dot(lx[0:N2, :], w_b[...])
        put_data(
            u1.at[i // 2], both[:, 0:N3] + both[:, N3:], pl.multiple_of(lax.rem(i, 2) * N3, N3)
        )

    loads[2].wait()

    @pl.loop(0, N2 // N3)
    def _(n):
        at = pl.multiple_of(n * N3, N3)
        put_weight(w_b2t, b2[:, pl.ds(at, N3)].T, at)

    for pair in range(PAIRS):
        out = dot(w_b2t[...], u1[pair])
        u2[:, 2 * pair, :] = out[:, 0:N3]
        u2[:, 2 * pair + 1, :] = out[:, N3:]

    @pl.when(jnp.logical_or(ka == 0, ka == BLOCKS - 1))
    def _():
        pl.semaphore_wait(barrier, PEERS)

    @pl.when(jnp.logical_and(ka > 0, ka < BLOCKS - 1))
    def _():
        pl.semaphore_wait(barrier, PEERS + 1)

    for g in range(GROUPS):

        def send(p, g=g):
            pltpu.make_async_remote_copy(
                u2.at[pl.ds(g * SPAN + p * OWN, OWN)],
                cols.at[g, :, pl.ds(pl.multiple_of(me * ROWS, ROWS), ROWS), :],
                fwd_send.at[g],
                fwd_recv.at[g],
                device_id=(p, ka),
                device_id_type=MESH,
            ).start()

        each_peer(send)
        pltpu.make_async_copy(
            u2.at[pl.ds(g * SPAN + me * OWN, OWN)],
            cols.at[g, :, pl.ds(pl.multiple_of(me * ROWS, ROWS), ROWS), :],
            fwd_recv.at[g],
        ).start()

    loads[3].wait()

    @pl.loop(0, N1 // N3)
    def _(n):
        at = pl.multiple_of(n * N3, N3)
        put_weight(w_b1t, b1[:, pl.ds(at, N3)].T, at)
        put_weight(w_b1, b1[pl.ds(at, N3), :], at)

    for n in range(N1 // N3):
        lev1[n * N3 : (n + 1) * N3, :] = spread(levels_first[n : n + 1, :])

    loads[4].wait()

    @pl.loop(0, N1 // N3)
    def _(n):
        at = pl.multiple_of(n * N3, N3)
        put_weight(w_k1, k1[pl.ds(at, N3), :], at)

    loads[5].wait()
    loads[6].wait()
    kval = ka.astype(f32)
    reach = [math.sqrt((BLOCKS - 1) * BLOCKS - k * (k + 1)) for k in range(BLOCKS)]

    def by_block(values):
        out = f32(values[-1])
        for k in range(BLOCKS - 1):
            out = jnp.where(ka == k, f32(values[k]), out)
        return out

    coupled_up = by_block(reach)
    coupled_down = by_block([0.0] + reach[:-1])
    turned = b3[...].T
    exact = functools.partial(
        jnp.dot, preferred_element_type=f32, precision=lax.Precision.HIGHEST
    )
    high, low = split(turned)
    high_k, low_k = split(exact(turned, k3[...].T))
    w_a[0:N3, 0:N3] = high
    w_a[N3:, 0:N3] = high
    w_a[0:N3, N3:] = high_k
    w_a[N3:, N3:] = high_k
    w_al[:, 0:N3] = low
    w_al[:, N3:] = low_k
    w_b[0:N3, 0:N3] = high
    w_b[N3:, 0:N3] = high
    w_b[0:N3, N3:] = low
    high, low = split(exact(turned, cor[...].T) * coupled_up)
    w_v[0:N3, 0:N3] = high
    w_v[0:N3, N3:] = low
    w_vl[0:N3, :] = high
    high, low = split(exact(turned, cor[...]) * coupled_down)
    w_v[N3:, 0:N3] = high
    w_v[N3:, N3:] = low
    w_vl[N3:, :] = high

    for g in range(GROUPS):
        put_weight(w_b2.at[g], b2[:, g * SPAN : (g + 1) * SPAN])
    loads[7].wait()

    @pl.loop(0, N2 // N3)
    def _(n):
        at = pl.multiple_of(n * N3, N3)
        put_weight(w_b2t, k2[pl.ds(at, N3), :], at)

    for half in range(2):
        put_data(data, b2[:, half * 256 : half * 256 + 256], 0)
        out = dot(w_b2t[...], data[...])
        for n in range(256 // SPAN):
            put_weight(w_kb.at[half * (256 // SPAN) + n], out[:, n * SPAN : (n + 1) * SPAN])

    loads[8].wait()
    loads[9].wait()

    @pl.loop(0, N2 // N3)
    def _(n):
        at = pl.ds(pl.multiple_of(n * N3, N3), N3)
        factors = rot[:, at]
        for i in range(ROWS):
            factor = spread(factors[i : i + 1, :])
            wide[i, at, :] = factor
            diag[i, at, :] = pot[i, at, :] + kval * kval * factor - shift_energy

    @pl.when(ka == 0)
    def _():
        below[...] = jnp.zeros(below.shape, f32)

    @pl.when(ka == BLOCKS - 1)
    def _():
        above[...] = jnp.zeros(above.shape, f32)

    for g in range(GROUPS):
        pltpu.make_async_copy(cols.at[g], cols.at[g], fwd_recv.at[g]).wait()
        for t in range(OWN):
            put_data(data, cols[g, t], t * N3)
        coeff = dot(w_b1t[...], data[...])
        for t in range(OWN):
            level = (
                lev1[...]
                + levels_second[g * SPAN + me * OWN + t]
                + levels_third[...]
                - shift_energy
            )
            filt = level / (level * level + damping * damping)
            put_data(data, coeff[:, t * N3 : (t + 1) * N3] * filt, t * N3)
        out = dot(w_b1[...], data[...])
        for t in range(OWN):
            part = out[:, t * N3 : (t + 1) * N3]
            xs[g, t] = part
            put_data(data, part, t * N3)

        def give(buffer, target, send_sem, recv_sem, g=g):
            def send(p):
                pltpu.make_async_remote_copy(
                    buffer.at[g, :, pl.ds(pl.multiple_of(p * ROWS, ROWS), ROWS), :],
                    target.at[pl.ds(g * SPAN + me * OWN, OWN)],
                    send_sem.at[g],
                    recv_sem.at[g],
                    device_id=(p, ka),
                    device_id_type=MESH,
                ).start()

            each_peer(send)
            pltpu.make_async_copy(
                buffer.at[g, :, pl.ds(pl.multiple_of(me * ROWS, ROWS), ROWS), :],
                target.at[pl.ds(g * SPAN + me * OWN, OWN)],
                recv_sem.at[g],
            ).start()

        give(xs, xr, x_send, x_recv)
        out = dot(w_k1[...], data[...])
        for t in range(OWN):
            ys[g, t] = out[:, t * N3 : (t + 1) * N3]
        give(ys, yr, y_send, y_recv)

    for g in range(GROUPS):
        rows = pl.ds(g * SPAN, SPAN)
        pltpu.make_async_copy(xr.at[rows], xr.at[rows], x_recv.at[g]).wait()

        @pl.when(ka > 0)
        def _(g=g, rows=rows):
            pltpu.make_async_remote_copy(
                xr.at[rows],
                above.at[rows],
                up_send.at[g],
                up_recv.at[g],
                device_id=(me, ka - 1),
                device_id_type=MESH,
            ).start()

        @pl.when(ka < BLOCKS - 1)
        def _(g=g, rows=rows):
            pltpu.make_async_remote_copy(
                xr.at[rows],
                below.at[rows],
                down_send.at[g],
                down_recv.at[g],
                device_id=(me, ka + 1),
                device_id_type=MESH,
            ).start()

        for i in range(ROWS):
            high, low = split(xr[rows, i, :])
            lx[i * SPAN : (i + 1) * SPAN, 0:N3] = high
            lx[i * SPAN : (i + 1) * SPAN, N3:] = low
        pltpu.make_async_copy(yr.at[rows], yr.at[rows], y_recv.at[g]).wait()
        for i in range(ROWS):
            high, low = split(yr[rows, i, :])
            ly[i * SPAN : (i + 1) * SPAN, 0:N3] = high
            ly[i * SPAN : (i + 1) * SPAN, N3:] = low

        @pl.loop(0, PAIRS)
        def _(pair):
            for t in range(2):
                at = pl.ds(pl.multiple_of((2 * pair + t) * SPAN, SPAN), SPAN)
                here = dot(lx[at, :], w_a[...]) + dot(lx[at, 0:N3], w_al[...])
                bent = dot(ly[at, :], w_b[...])
                put_data(t1.at[pair], here[:, 0:N3], t * N3)
                put_data(t2.at[pair], here[:, N3:] + bent[:, 0:N3] + bent[:, N3:], t * N3)
            out = dot(w_b2[g], t1[pair])
            other = dot(w_b2[g], t2[pair]) + dot(w_kb[g], t1[pair])
            for t in range(2):
                lanes = slice(t * N3, (t + 1) * N3)
                if g == 0:
                    src_out = out[:, lanes]
                    pot[2 * pair + t] = src_out
                    acc_p[2 * pair + t] = other[:, lanes]
                else:
                    pot[2 * pair + t] += out[:, lanes]
                    acc_p[2 * pair + t] += other[:, lanes]

        @pl.when(ka < BLOCKS - 1)
        def _(g=g, rows=rows):
            pltpu.make_async_copy(above.at[rows], above.at[rows], up_recv.at[g]).wait()

        @pl.when(ka > 0)
        def _(g=g, rows=rows):
            pltpu.make_async_copy(below.at[rows], below.at[rows], down_recv.at[g]).wait()

        for i in range(ROWS):
            at = slice(i * SPAN, (i + 1) * SPAN)
            high, low = split(above[rows, i, :])
            lx[at, 0:N3] = high
            ly[at, 0:N3] = low
            high, low = split(below[rows, i, :])
            lx[at, N3:] = high
            ly[at, N3:] = low

        @pl.loop(0, PAIRS)
        def _(pair):
            for t in range(2):
                at = pl.ds(pl.multiple_of((2 * pair + t) * SPAN, SPAN), SPAN)
                mixed = dot(lx[at, :], w_v[...])
                put_data(
                    tv.at[pair],
                    mixed[:, 0:N3] + mixed[:, N3:] + dot(ly[at, :], w_vl[...]),
                    t * N3,
                )
            out = dot(w_b2[g], tv[pair])
            for t in range(2):
                lanes = slice(t * N3, (t + 1) * N3)
                if g == 0:
                    acc_v[2 * pair + t] = out[:, lanes]
                elif g < GROUPS - 1:
                    acc_v[2 * pair + t] += out[:, lanes]
                else:
                    i = 2 * pair + t
                    solved = pot[i]
                    applied = (
                        acc_p[i] + diag[i] * solved + wide[i] * (acc_v[i] + out[:, lanes])
                    )
                    src[i] = src[i] - applied

        if g == GROUPS - 1:
            results = []
            for n, (source, target) in enumerate(((pot, solved_out), (src, residual_out))):
                copy = pltpu.make_async_copy(source, target.at[0], out_sem.at[n])
                copy.start()
                results.append(copy)
            for copy in results:
                copy.wait()

    sent = pl.ds(0, (PEERS - 1) * ROWS)
    for g in range(GROUPS):
        rows = pl.ds(g * SPAN, SPAN)
        part = u2.at[pl.ds(0, (PEERS - 1) * OWN)]
        pltpu.make_async_copy(part, part, fwd_send.at[g]).wait()
        part = xs.at[g, :, sent, :]
        pltpu.make_async_copy(part, part, x_send.at[g]).wait()
        part = ys.at[g, :, sent, :]
        pltpu.make_async_copy(part, part, y_send.at[g]).wait()

        @pl.when(ka > 0)
        def _(g=g, rows=rows):
            pltpu.make_async_copy(xr.at[rows], xr.at[rows], up_send.at[g]).wait()

        @pl.when(ka < BLOCKS - 1)
        def _(g=g, rows=rows):
            pltpu.make_async_copy(xr.at[rows], xr.at[rows], down_send.at[g]).wait()


def per_device(
    states,
    potential,
    rotation_factor,
    basis_first,
    basis_second,
    basis_third,
    levels_first,
    levels_second,
    levels_third,
    kinetic_first,
    kinetic_second,
    kinetic_third,
    coriolis_matrix,
):
    vmem, dma = pltpu.VMEM, pltpu.SemaphoreType.DMA
    anywhere = pl.BlockSpec(memory_space=pl.ANY)
    here = pl.BlockSpec(memory_space=pltpu.VMEM)
    slab = (ROWS, N2, N3)
    turned = (N2, ROWS, N3)
    columns = (GROUPS, OWN, N1, N3)
    weight = vmem((N1, 3 * N1), bf16)
    parts = vmem((GROUPS, N2, 3 * SPAN), bf16)
    stacked = vmem((PAIRS, 3 * SPAN, 2 * N3), bf16)
    square = vmem((N1, N1), f32)
    small = vmem((N3, N3), f32)
    scratch = [
        vmem(slab, f32),
        vmem(slab, f32),
        vmem((ROWS, N2), f32),
        square,
        square,
        square,
        square,
        small,
        small,
        small,
        weight,
        weight,
        weight,
        weight,
        parts,
        parts,
        vmem((PAIRS, 3 * N2, 2 * N3), bf16),
        vmem(turned, f32),
        vmem(columns, f32),
        vmem(columns, f32),
        vmem(columns, f32),
        vmem(turned, f32),
        vmem(turned, f32),
        vmem(turned, f32),
        vmem(turned, f32),
        vmem((3 * N1, OWN * N3), bf16),
        vmem((ROWS * SPAN, 2 * N3), bf16),
        vmem((ROWS * SPAN, 2 * N3), bf16),
        stacked,
        stacked,
        stacked,
        vmem((2 * N3, 2 * N3), bf16),
        vmem((N3, 2 * N3), bf16),
        vmem((2 * N3, 2 * N3), bf16),
        vmem((2 * N3, 2 * N3), bf16),
        vmem((2 * N3, N3), bf16),
        vmem(slab, f32),
        vmem(slab, f32),
        vmem(slab, f32),
        vmem(slab, f32),
        vmem((N1, N3), f32),
        dma((10,)),
        dma((2,)),
    ] + [dma((GROUPS,))] * 10
    return pl.pallas_call(
        kernel,
        out_shape=(
            jax.ShapeDtypeStruct((1,) + slab, f32),
            jax.ShapeDtypeStruct((1,) + slab, f32),
        ),
        in_specs=[anywhere] * 6
        + [here, pl.BlockSpec(memory_space=pltpu.SMEM), here]
        + [anywhere] * 4,
        out_specs=(anywhere, anywhere),
        scratch_shapes=scratch,
        compiler_params=pltpu.CompilerParams(
            collective_id=0, has_side_effects=True, vmem_limit_bytes=66_000_000
        ),
        name="filter_step",
    )(
        states,
        potential,
        rotation_factor,
        basis_first,
        basis_second,
        basis_third,
        levels_first.reshape(N1 // N3, N3),
        levels_second,
        levels_third.reshape(1, N3),
        kinetic_first,
        kinetic_second,
        kinetic_third,
        coriolis_matrix,
    )


def solution(mesh):
    return jax.shard_map(
        per_device,
        mesh=mesh,
        in_specs=(
            P("ka", "coord", None, None),
            P("coord", None, None),
            P("coord", None),
            P(),
            P(),
            P(),
            P(),
            P(),
            P(),
            P(),
            P(),
            P(),
            P(),
        ),
        out_specs=(P("ka", "coord", None, None), P("ka", "coord", None, None)),
        check_vma=False,
    )
```

```python
import functools
import math

import jax
import jax.numpy as jnp
from jax import lax
from jax.experimental import pallas as pl
from jax.experimental.pallas import tpu as pltpu
from jax.sharding import PartitionSpec as P

MESH = pl.DeviceIdType.MESH
f32 = jnp.float32
bf16 = jnp.bfloat16
shift_energy = 2.5
damping = 0.5

PEERS = 64
BLOCKS = 4
GROUPS = 4
N1 = 512
N2 = 512
N3 = 128
ROWS = N1 // PEERS
PAIRS = ROWS // 2
SPAN = N2 // GROUPS
OWN = 4
HALVES = OWN // 2
PLANES = 8
NEAR = 4
LINES = PEERS // PLANES
SERVED = NEAR * LINES


def split(value):
    high = value.astype(bf16)
    return high, (value - high.astype(f32)).astype(bf16)


def dot(left, right):
    return jnp.dot(left, right, preferred_element_type=f32)


def put_weight(ref, value, offset=0, base=0):
    high, low = split(value)
    width = value.shape[1]
    for place, part in enumerate((high, low, high)):
        lanes = pl.ds(pl.multiple_of(base + place * width, N3), width)
        ref[pl.ds(offset, value.shape[0]), lanes] = part


def put_data(ref, value, lane, base=0):
    high, low = split(value)
    height, width = value.shape
    for place, part in enumerate((high, high, low)):
        rows = pl.ds(pl.multiple_of(base + place * height, N3), height)
        ref[rows, pl.ds(lane, width)] = part


def spread(row, height=N3):
    return jnp.broadcast_to(row, (height, row.shape[1])).T


def kernel(
    states,
    potential,
    rotation,
    first,
    second,
    third,
    levels_first,
    levels_second,
    levels_third,
    kin_first,
    kin_second,
    kin_third,
    coriolis,
    solved_out,
    residual_out,
    src,
    pot,
    rot,
    b1,
    b2,
    k1,
    k2,
    b3,
    k3,
    cor,
    w_b2t,
    w_b1t,
    w_tmp,
    w_xy,
    w_b2,
    w_kb,
    u1,
    u2,
    cols,
    xs,
    ys,
    xr,
    yr,
    above,
    below,
    data,
    lx,
    ly,
    t1,
    t2,
    tv,
    angular,
    w_c,
    w_a,
    w_al,
    w_b,
    w_v,
    w_vl,
    acc_v,
    diag,
    wide,
    lev1,
    picked,
    load_sem,
    out_sem,
    fwd_send,
    fwd_recv,
    hand_send,
    hand_recv,
    x_send,
    x_recv,
    y_send,
    y_recv,
    up_send,
    up_recv,
    down_send,
    down_recv,
):
    me = lax.axis_index("coord")
    ka = lax.axis_index("ka")
    my_y, my_x, my_z = me // 16, lax.rem(me // 8, 2), lax.rem(me, 8)
    my_line = me // PLANES

    def side(g):
        return lax.rem(my_z + lax.rem(g, 2), 2)

    def pair_of(g):
        return lax.rem(my_z - lax.rem(g, 2) + PLANES, PLANES) // 2

    def near_plane(g, n):
        return lax.rem(my_z + (2 * side(g) - 1) * n + PLANES, PLANES)

    def line(step):
        return lax.rem(my_y + step // 2, 4) * 2 + lax.rem(my_x + step, 2)

    def loop(start, stop, body):
        def step(s, carry):
            body(s)
            return carry

        lax.fori_loop(start, stop, step, 0)

    loads = [
        pltpu.make_async_copy(source, target, load_sem.at[index])
        for index, (source, target) in enumerate(
            (
                (second, b2),
                (states.at[0], src),
                (third, b3),
                (first, b1),
                (kin_first, k1),
                (kin_third, k3),
                (coriolis, cor),
                (kin_second, k2),
                (potential, pot),
                (rotation, rot),
            )
        )
    ]
    for copy in loads[:2]:
        copy.start()
    barrier = pltpu.get_barrier_semaphore()
    def greet(s):
        p = line(s // PLANES) * PLANES + lax.rem(my_z + s, PLANES)
        pl.semaphore_signal(barrier, inc=1, device_id=(p, ka), device_id_type=MESH)

    loop(1, PEERS, greet)

    @pl.when(ka > 0)
    def _():
        pl.semaphore_signal(barrier, inc=1, device_id=(me, ka - 1), device_id_type=MESH)

    @pl.when(ka < BLOCKS - 1)
    def _():
        pl.semaphore_signal(barrier, inc=1, device_id=(me, ka + 1), device_id_type=MESH)

    loads[0].wait()

    loads[1].wait()
    for copy in loads[2:]:
        copy.start()

    @pl.loop(0, PAIRS)
    def _(pair):
        for t in range(2):
            put_data(u1.at[pair], src[2 * pair + t], t * N3)

    def way_out(g):
        rows = pl.ds(pl.multiple_of(g * SPAN, SPAN), SPAN)
        put_weight(w_b2t, b2[:, rows].T)
        for pair in range(PAIRS):
            out = dot(w_b2t[...], u1[pair])
            u2[rows, 2 * pair, :] = out[:, 0:N3]
            u2[rows, 2 * pair + 1, :] = out[:, N3:]

        @pl.when(g == 0)
        def _():
            @pl.when(jnp.logical_or(ka == 0, ka == BLOCKS - 1))
            def _():
                pl.semaphore_wait(barrier, PEERS)

            @pl.when(jnp.logical_and(ka > 0, ka < BLOCKS - 1))
            def _():
                pl.semaphore_wait(barrier, PEERS + 1)

        turn = lax.rem(g, 2)

        def place(s):
            where = line(s // 4)
            pair = lax.rem(pair_of(g) + s, 4)
            away = lax.rem(my_z - turn - 2 * pair + 2 * PLANES, PLANES)
            upper = jnp.logical_and(away >= 1, away <= NEAR).astype(jnp.int32)
            plane = lax.rem(2 * pair + upper + turn, PLANES)
            return g * SPAN + (where * 4 + pair) * OWN, where * PLANES + plane

        def send(s):
            column, p = place(s)
            pltpu.make_async_remote_copy(
                u2.at[pl.ds(column, OWN)],
                cols.at[g, :, my_line, my_z],
                fwd_send.at[g],
                fwd_recv.at[g],
                device_id=(p, ka),
                device_id_type=MESH,
            ).start()

        loop(1, SERVED, send)
        pltpu.make_async_copy(
            u2.at[pl.ds(place(0)[0], OWN)], cols.at[g, :, my_line, my_z], fwd_recv.at[g]
        ).start()

    def hand_over(g):
        pltpu.make_async_copy(cols.at[g, 0:HALVES], cols.at[g, 0:HALVES], fwd_recv.at[g]).wait()
        partner = lax.rem(my_z + 1 - 2 * side(g) + PLANES, PLANES)
        for n in range(NEAR):
            part = cols.at[g, :, :, near_plane(g, n)]
            pltpu.make_async_remote_copy(
                part,
                part,
                hand_send.at[g],
                hand_recv.at[g],
                device_id=(my_line * PLANES + partner, ka),
                device_id_type=MESH,
            ).start()

    def give(g, buffer, target, send_sem, recv_sem):
        home = pl.ds(g * SPAN + (my_line * 4 + pair_of(g)) * OWN, OWN)

        def send(s):
            where, n = line(s // NEAR), lax.rem(s, NEAR)
            pltpu.make_async_remote_copy(
                buffer.at[g, :, n, where],
                target.at[home],
                send_sem.at[g],
                recv_sem.at[g],
                device_id=(where * PLANES + near_plane(g, n), ka),
                device_id_type=MESH,
            ).start()

        loop(1, SERVED, send)
        pltpu.make_async_copy(
            buffer.at[g, :, 0, my_line], target.at[home], recv_sem.at[g]
        ).start()

    def in_columns(g):
        pltpu.make_async_copy(cols.at[g, 0:HALVES], cols.at[g, 0:HALVES], hand_recv.at[g]).wait()

        @pl.loop(0, HALVES)
        def _(half):
            for t in range(2):
                high, low = split(cols[g, 2 * half + t].reshape(N1, N3))
                lx[0:N1, 0:N3] = high
                lx[0:N1, N3:] = low
                both = dot(lx[0:N1, :], w_c[...])
                put_data(data, both[:, 0:N3] + both[:, N3:], t * N3)
            coeff = dot(w_b1t[...], data[...])
            for t in range(2):
                column = g * SPAN + (my_line * 4 + pair_of(g)) * OWN + 2 * half + t
                level = (
                    lev1[...] + levels_second[column] + levels_third[...] - shift_energy
                )
                filt = level / (level * level + damping * damping)
                put_data(data, coeff[:, t * N3 : (t + 1) * N3] * filt, t * N3)
            out = dot(w_xy[lax.rem(g, 2)], data[...])
            for t in range(2):
                part = out[:, t * N3 : (t + 1) * N3].reshape(2, NEAR, LINES, ROWS, N3)
                xs[g, 2 * half + t] = part[0]
                ys[g, 2 * half + t] = part[1]

        give(g, xs, xr, x_send, x_recv)

    def give_bent(g):
        give(g, ys, yr, y_send, y_recv)

    def in_slab(g):
        rows = pl.ds(pl.multiple_of(g * SPAN, SPAN), SPAN)
        pltpu.make_async_copy(xr.at[rows], xr.at[rows], x_recv.at[g]).wait()

        @pl.when(ka > 0)
        def _():
            pltpu.make_async_remote_copy(
                xr.at[rows],
                above.at[rows],
                up_send.at[g],
                up_recv.at[g],
                device_id=(me, ka - 1),
                device_id_type=MESH,
            ).start()

        @pl.when(ka < BLOCKS - 1)
        def _():
            pltpu.make_async_remote_copy(
                xr.at[rows],
                below.at[rows],
                down_send.at[g],
                down_recv.at[g],
                device_id=(me, ka + 1),
                device_id_type=MESH,
            ).start()

        @pl.when(g > 0)
        def _():
            give_bent(g - 1)

        @pl.when(g == GROUPS - 1)
        def _():
            give_bent(g)

        for i in range(ROWS):
            high, low = split(xr[rows, i, :])
            lx[i * SPAN : (i + 1) * SPAN, 0:N3] = high
            lx[i * SPAN : (i + 1) * SPAN, N3:] = low

        @pl.loop(0, PAIRS)
        def _(pair):
            for t in range(2):
                at = pl.ds(pl.multiple_of((2 * pair + t) * SPAN, SPAN), SPAN)
                here = dot(lx[at, :], w_a[...]) + dot(lx[at, 0:N3], w_al[...])
                put_data(t1.at[pair], here[:, 0:N3], t * N3, lax.rem(g, 2) * 3 * SPAN)
                angular[2 * pair + t, rows, :] = here[:, N3:]

        @pl.when(lax.rem(g, 2) == 1)
        def _():
            both = pl.ds(pl.multiple_of(g // 2 * 6 * SPAN, 6 * SPAN), 6 * SPAN)

            @pl.loop(0, PAIRS)
            def _(pair):
                out = dot(w_b2[:, both], t1[pair])
                for t in range(2):
                    pot[2 * pair + t] += out[:, t * N3 : (t + 1) * N3]
                out = dot(w_kb[:, both], t1[pair])
                for t in range(2):
                    src[2 * pair + t] -= out[:, t * N3 : (t + 1) * N3]

    def between_blocks(g, last=False):
        rows = pl.ds(pl.multiple_of(g * SPAN, SPAN), SPAN)

        @pl.when(ka < BLOCKS - 1)
        def _():
            pltpu.make_async_copy(above.at[rows], above.at[rows], up_recv.at[g]).wait()

        @pl.when(ka > 0)
        def _():
            pltpu.make_async_copy(below.at[rows], below.at[rows], down_recv.at[g]).wait()

        for i in range(ROWS):
            at = slice(i * SPAN, (i + 1) * SPAN)
            high, low = split(above[rows, i, :])
            lx[at, 0:N3] = high
            ly[at, 0:N3] = low
            high, low = split(below[rows, i, :])
            lx[at, N3:] = high
            ly[at, N3:] = low

        @pl.loop(0, PAIRS)
        def _(pair):
            for t in range(2):
                at = pl.ds(pl.multiple_of((2 * pair + t) * SPAN, SPAN), SPAN)
                mixed = dot(lx[at, :], w_v[...])
                mixed = mixed[:, 0:N3] + mixed[:, N3:] + dot(ly[at, :], w_vl[...])
                put_data(tv.at[pair], mixed, t * N3, lax.rem(g, 2) * 3 * SPAN)

        @pl.when(lax.rem(g, 2) == 1)
        def _():
            both = pl.ds(pl.multiple_of(g // 2 * 6 * SPAN, 6 * SPAN), 6 * SPAN)

            @pl.loop(0, PAIRS)
            def _(pair):
                out = dot(w_b2[:, both], tv[pair])
                for t in range(2):
                    acc_v[2 * pair + t] += out[:, t * N3 : (t + 1) * N3]
                if last:
                    two = pl.ds(2 * pair, 2)
                    src[two] -= wide[two] * acc_v[two]
                    pltpu.make_async_copy(
                        src.at[two], residual_out.at[0, two], out_sem.at[1]
                    ).start()

    way_out(0)

    @pl.loop(0, 2 * GROUPS - 1)
    def _(step):
        @pl.when(step == 0)
        def _():
            way_out(1)

            loads[2].wait()
            high, low = split(b3[...])
            w_c[0:N3, 0:N3] = high
            w_c[N3:, 0:N3] = high
            w_c[0:N3, N3:] = low
            w_c[N3:, N3:] = jnp.zeros((N3, N3), bf16)
            loads[3].wait()

            @pl.loop(0, N1 // N3)
            def _(n):
                at = pl.multiple_of(n * N3, N3)
                put_weight(w_b1t, b1[:, pl.ds(at, N3)].T, at)

            for n in range(N1 // N3):
                lev1[n * N3 : (n + 1) * N3, :] = spread(levels_first[n : n + 1, :])


        @pl.when(step < GROUPS)
        def _():
            hand_over(step)

        @pl.when(step < GROUPS - 2)
        def _():
            way_out(step + 2)

        @pl.when(step == 0)
        def _():
            loads[4].wait()

            for turn in range(2):

                def gather(s, turn=turn):
                    start = pl.multiple_of(
                        lax.rem(s, LINES) * PLANES * ROWS + near_plane(turn, s // LINES) * ROWS, ROWS
                    )
                    to = pl.multiple_of(s * ROWS, ROWS)
                    picked[pl.ds(to, ROWS), :] = b1[pl.ds(start, ROWS), :]
                    picked[pl.ds(N1 // 2 + to, ROWS), :] = k1[pl.ds(start, ROWS), :]

                loop(0, SERVED, gather)

                @pl.loop(0, 2)
                def _(half, turn=turn):
                    at = pl.multiple_of(half * N3, N3)
                    put_weight(w_xy.at[turn], picked[pl.ds(at, N3), :], at)
                    put_weight(w_tmp, picked[pl.ds(N1 // 2 + at, N3), :], at)

                @pl.loop(0, 2)
                def _(half):
                    at = pl.ds(pl.multiple_of(half * 256, 256), 256)
                    put_data(data, b1[:, at], 0)
                    picked[N1 // 2 :, at] = dot(w_tmp[0 : N1 // 2, :], data[...])

                @pl.loop(0, 2)
                def _(half, turn=turn):
                    at = pl.multiple_of(N1 // 2 + half * N3, N3)
                    put_weight(w_xy.at[turn], picked[pl.ds(at, N3), :], at)


        @pl.when(step == 1)
        def _():
            loads[5].wait()
            loads[6].wait()
            kval = ka.astype(f32)
            reach = [math.sqrt((BLOCKS - 1) * BLOCKS - k * (k + 1)) for k in range(BLOCKS)]

            def by_block(values):
                out = f32(values[-1])
                for k in range(BLOCKS - 1):
                    out = jnp.where(ka == k, f32(values[k]), out)
                return out

            coupled_up = by_block(reach)
            coupled_down = by_block([0.0] + reach[:-1])
            turned = b3[...].T
            exact = functools.partial(
                jnp.dot, preferred_element_type=f32, precision=lax.Precision.HIGHEST
            )
            high, low = split(turned)
            high_k, low_k = split(exact(turned, k3[...].T))
            w_a[0:N3, 0:N3] = high
            w_a[N3:, 0:N3] = high
            w_a[0:N3, N3:] = high_k
            w_a[N3:, N3:] = high_k
            w_al[:, 0:N3] = low
            w_al[:, N3:] = low_k
            w_b[0:N3, 0:N3] = high
            w_b[N3:, 0:N3] = high
            w_b[0:N3, N3:] = low
            w_b[N3:, N3:] = jnp.zeros((N3, N3), bf16)
            high, low = split(exact(turned, cor[...].T) * coupled_up)
            w_v[0:N3, 0:N3] = high
            w_v[0:N3, N3:] = low
            w_vl[0:N3, :] = high
            high, low = split(exact(turned, cor[...]) * coupled_down)
            w_v[N3:, 0:N3] = high
            w_v[N3:, N3:] = low
            w_vl[N3:, :] = high

            @pl.loop(0, GROUPS)
            def _(g):
                part = b2[:, pl.ds(pl.multiple_of(g * SPAN, SPAN), SPAN)]
                put_weight(w_b2, part, 0, g * 3 * SPAN)

            loads[7].wait()

            @pl.loop(0, N2 // N3)
            def _(n):
                at = pl.multiple_of(n * N3, N3)
                put_weight(w_tmp, k2[pl.ds(at, N3), :], at)

            @pl.loop(0, 2)
            def _(half):
                put_data(data, b2[:, pl.ds(pl.multiple_of(half * 256, 256), 256)], 0)
                out = dot(w_tmp[...], data[...])
                for n in range(256 // SPAN):
                    part = out[:, n * SPAN : (n + 1) * SPAN]
                    put_weight(w_kb, part, 0, (half * (256 // SPAN) + n) * 3 * SPAN)

            loads[8].wait()
            loads[9].wait()

            @pl.loop(0, N2 // N3)
            def _(n):
                at = pl.ds(pl.multiple_of(n * N3, N3), N3)
                factors = rot[:, at]
                for i in range(ROWS):
                    factor = spread(factors[i : i + 1, :])
                    wide[i, at, :] = factor
                    diag[i, at, :] = pot[i, at, :] + kval * kval * factor - shift_energy
                    pot[i, at, :] = jnp.zeros((N3, N3), f32)
                    acc_v[i, at, :] = jnp.zeros((N3, N3), f32)

            @pl.when(ka == 0)
            def _():
                below[...] = jnp.zeros(below.shape, f32)

            @pl.when(ka == BLOCKS - 1)
            def _():
                above[...] = jnp.zeros(above.shape, f32)


        @pl.when(jnp.logical_and(step >= 1, step <= GROUPS))
        def _():
            in_columns(step - 1)

        @pl.when(step >= GROUPS - 1)
        def _():
            in_slab(step - GROUPS + 1)

        @pl.when(step > GROUPS)
        def _():
            between_blocks(step - GROUPS - 1)

    results = [pltpu.make_async_copy(pot, solved_out.at[0], out_sem.at[0])]
    results[0].start()
    between_blocks(GROUPS - 2)

    @pl.loop(0, ROWS)
    def _(i):
        src[i] -= diag[i] * pot[i]

    @pl.loop(0, GROUPS)
    def _(g):
        rows = pl.ds(pl.multiple_of(g * SPAN, SPAN), SPAN)
        pltpu.make_async_copy(yr.at[rows], yr.at[rows], y_recv.at[g]).wait()
        for i in range(ROWS):
            high, low = split(yr[rows, i, :])
            ly[i * SPAN : (i + 1) * SPAN, 0:N3] = high
            ly[i * SPAN : (i + 1) * SPAN, N3:] = low

        @pl.loop(0, PAIRS)
        def _(pair):
            for t in range(2):
                at = pl.ds(pl.multiple_of((2 * pair + t) * SPAN, SPAN), SPAN)
                bent = dot(ly[at, :], w_b[...])
                bent = bent[:, 0:N3] + bent[:, N3:] + angular[2 * pair + t, rows, :]
                put_data(t2.at[pair], bent, t * N3)
            each = pl.ds(pl.multiple_of(g * 3 * SPAN, 3 * SPAN), 3 * SPAN)
            out = dot(w_b2[:, each], t2[pair])
            for t in range(2):
                src[2 * pair + t] -= out[:, t * N3 : (t + 1) * N3]

    between_blocks(GROUPS - 1, last=True)
    results.append(pltpu.make_async_copy(src, residual_out.at[0], out_sem.at[1]))

    @pl.loop(0, GROUPS)
    def _(g):
        rows = pl.ds(g * SPAN, SPAN)
        part = u2.at[pl.ds(0, (SERVED - 1) * OWN)]
        pltpu.make_async_copy(part, part, fwd_send.at[g]).wait()
        pltpu.make_async_copy(part, part, x_send.at[g]).wait()
        pltpu.make_async_copy(part, part, y_send.at[g]).wait()
        pltpu.make_async_copy(cols.at[g, 0:HALVES], cols.at[g, 0:HALVES], hand_send.at[g]).wait()

        @pl.when(ka > 0)
        def _():
            pltpu.make_async_copy(xr.at[rows], xr.at[rows], up_send.at[g]).wait()

        @pl.when(ka < BLOCKS - 1)
        def _():
            pltpu.make_async_copy(xr.at[rows], xr.at[rows], down_send.at[g]).wait()

    for copy in results:
        copy.wait()


def per_device(
    states,
    potential,
    rotation_factor,
    basis_first,
    basis_second,
    basis_third,
    levels_first,
    levels_second,
    levels_third,
    kinetic_first,
    kinetic_second,
    kinetic_third,
    coriolis_matrix,
):
    vmem, dma = pltpu.VMEM, pltpu.SemaphoreType.DMA
    anywhere = pl.BlockSpec(memory_space=pl.ANY)
    here = pl.BlockSpec(memory_space=pltpu.VMEM)
    slab = (ROWS, N2, N3)
    turned = (N2, ROWS, N3)
    columns = (GROUPS, OWN, LINES, PLANES, ROWS, N3)
    given = (GROUPS, OWN, NEAR, LINES, ROWS, N3)
    weight = vmem((N1, 3 * N1), bf16)
    parts = vmem((N2, GROUPS * 3 * SPAN), bf16)
    stacked = vmem((PAIRS, 6 * SPAN, 2 * N3), bf16)
    square = vmem((N1, N1), f32)
    small = vmem((N3, N3), f32)
    scratch = [
        vmem(slab, f32),
        vmem(slab, f32),
        vmem((ROWS, N2), f32),
        square,
        square,
        square,
        square,
        small,
        small,
        small,
        vmem((SPAN, 3 * N2), bf16),
        weight,
        weight,
        vmem((2, N1, 3 * N1), bf16),
        parts,
        parts,
        vmem((PAIRS, 3 * N2, 2 * N3), bf16),
        vmem(turned, f32),
        vmem(columns, f32),
        vmem(given, f32),
        vmem(given, f32),
        vmem(turned, f32),
        vmem(turned, f32),
        vmem(turned, f32),
        vmem(turned, f32),
        vmem((3 * N1, 2 * N3), bf16),
        vmem((ROWS * SPAN, 2 * N3), bf16),
        vmem((ROWS * SPAN, 2 * N3), bf16),
        stacked,
        vmem((PAIRS, 3 * SPAN, 2 * N3), bf16),
        stacked,
        vmem(slab, f32),
        vmem((2 * N3, 2 * N3), bf16),
        vmem((2 * N3, 2 * N3), bf16),
        vmem((N3, 2 * N3), bf16),
        vmem((2 * N3, 2 * N3), bf16),
        vmem((2 * N3, 2 * N3), bf16),
        vmem((2 * N3, N3), bf16),
        vmem(slab, f32),
        vmem(slab, f32),
        vmem(slab, f32),
        vmem((N1, N3), f32),
        square,
        dma((10,)),
        dma((2,)),
    ] + [dma((GROUPS,))] * 12
    return pl.pallas_call(
        kernel,
        out_shape=(
            jax.ShapeDtypeStruct((1,) + slab, f32),
            jax.ShapeDtypeStruct((1,) + slab, f32),
        ),
        in_specs=[anywhere] * 6
        + [here, pl.BlockSpec(memory_space=pltpu.SMEM), here]
        + [anywhere] * 4,
        out_specs=(anywhere, anywhere),
        scratch_shapes=scratch,
        compiler_params=pltpu.CompilerParams(
            collective_id=0, has_side_effects=True, vmem_limit_bytes=66_000_000
        ),
        name="filter_step",
    )(
        states,
        potential,
        rotation_factor,
        basis_first,
        basis_second,
        basis_third,
        levels_first.reshape(N1 // N3, N3),
        levels_second,
        levels_third.reshape(1, N3),
        kinetic_first,
        kinetic_second,
        kinetic_third,
        coriolis_matrix,
    )


def solution(mesh):
    return jax.shard_map(
        per_device,
        mesh=mesh,
        in_specs=(
            P("ka", "coord", None, None),
            P("coord", None, None),
            P("coord", None),
            P(),
            P(),
            P(),
            P(),
            P(),
            P(),
            P(),
            P(),
            P(),
            P(),
        ),
        out_specs=(P("ka", "coord", None, None), P("ka", "coord", None, None)),
        check_vma=False,
    )
```

```python
import functools
import math

import jax
import jax.numpy as jnp
from jax import lax
from jax.experimental import pallas as pl
from jax.experimental.pallas import tpu as pltpu
from jax.sharding import PartitionSpec as P

MESH = pl.DeviceIdType.MESH
f32 = jnp.float32
bf16 = jnp.bfloat16
shift_energy = 2.5
damping = 0.5

PEERS = 64
BLOCKS = 4
GROUPS = 4
N1 = 512
N2 = 512
N3 = 128
ROWS = N1 // PEERS
PAIRS = ROWS // 2
SPAN = N2 // GROUPS
OWN = 4
HALVES = OWN // 2
PLANES = 8
NEAR = 4
LINES = PEERS // PLANES
SERVED = NEAR * LINES


def split(value):
    high = value.astype(bf16)
    return high, (value - high.astype(f32)).astype(bf16)


def dot(left, right):
    return jnp.dot(left, right, preferred_element_type=f32)


def put_weight(ref, value, offset=0, base=0):
    high, low = split(value)
    width = value.shape[1]
    for place, part in enumerate((high, low, high)):
        lanes = pl.ds(pl.multiple_of(base + place * width, N3), width)
        ref[pl.ds(offset, value.shape[0]), lanes] = part


def put_data(ref, value, lane, base=0):
    high, low = split(value)
    height, width = value.shape
    for place, part in enumerate((high, high, low)):
        rows = pl.ds(pl.multiple_of(base + place * height, N3), height)
        ref[rows, pl.ds(lane, width)] = part


def spread(row, height=N3):
    return jnp.broadcast_to(row, (height, row.shape[1])).T


def kernel(
    states,
    potential,
    rotation,
    first,
    second,
    third,
    levels_first,
    levels_second,
    levels_third,
    kin_first,
    kin_second,
    kin_third,
    coriolis,
    solved_out,
    residual_out,
    src,
    pot,
    rot,
    b1,
    b2,
    k1,
    k2,
    b3,
    k3,
    cor,
    w_b2t,
    w_b1t,
    w_tmp,
    w_xy,
    w_b2,
    w_kb,
    u1,
    u2,
    cols,
    xs,
    ys,
    xr,
    yr,
    above,
    below,
    data,
    lx,
    ly,
    t1,
    t2,
    tv,
    angular,
    w_c,
    w_a,
    w_al,
    w_b,
    w_v,
    w_vl,
    acc_v,
    diag,
    wide,
    lev1,
    picked,
    load_sem,
    out_sem,
    fwd_send,
    fwd_recv,
    hand_send,
    hand_recv,
    x_send,
    x_recv,
    y_send,
    y_recv,
    up_send,
    up_recv,
    down_send,
    down_recv,
):
    me = lax.axis_index("coord")
    ka = lax.axis_index("ka")
    my_y, my_x, my_z = me // 16, lax.rem(me // 8, 2), lax.rem(me, 8)
    my_line = me // PLANES

    def side(g):
        return lax.rem(my_z + lax.rem(g, 2), 2)

    def pair_of(g):
        return lax.rem(my_z - lax.rem(g, 2) + PLANES, PLANES) // 2

    def near_plane(g, n):
        return lax.rem(my_z + (2 * side(g) - 1) * n + PLANES, PLANES)

    def line(step):
        return lax.rem(my_y + step // 2, 4) * 2 + lax.rem(my_x + step, 2)

    def loop(start, stop, body):
        def step(s, carry):
            body(s)
            return carry

        lax.fori_loop(start, stop, step, 0)

    loads = [
        pltpu.make_async_copy(source, target, load_sem.at[index])
        for index, (source, target) in enumerate(
            (
                (second, b2),
                (states.at[0], src),
                (third, b3),
                (first, b1),
                (kin_first, k1),
                (kin_third, k3),
                (coriolis, cor),
                (kin_second, k2),
                (potential, pot),
                (rotation, rot),
            )
        )
    ]
    for copy in loads[:2]:
        copy.start()
    barrier = pltpu.get_barrier_semaphore()
    def greet(s):
        p = line(s // PLANES) * PLANES + lax.rem(my_z + s, PLANES)
        pl.semaphore_signal(barrier, inc=1, device_id=(p, ka), device_id_type=MESH)

    loop(1, PEERS, greet)

    @pl.when(ka > 0)
    def _():
        pl.semaphore_signal(barrier, inc=1, device_id=(me, ka - 1), device_id_type=MESH)

    @pl.when(ka < BLOCKS - 1)
    def _():
        pl.semaphore_signal(barrier, inc=1, device_id=(me, ka + 1), device_id_type=MESH)

    loads[0].wait()

    loads[1].wait()
    for copy in loads[2:]:
        copy.start()

    @pl.loop(0, PAIRS)
    def _(pair):
        for t in range(2):
            put_data(u1.at[pair], src[2 * pair + t], t * N3)

    def strided(g, i):
        return pl.ds(g * SPAN * ROWS + i, SPAN, stride=ROWS)

    flat = (N2 * ROWS, N3)
    u2_flat, xr_flat, yr_flat = u2.reshape(flat), xr.reshape(flat), yr.reshape(flat)
    above_flat, below_flat = above.reshape(flat), below.reshape(flat)

    def way_out(g):
        rows = pl.ds(pl.multiple_of(g * SPAN, SPAN), SPAN)
        put_weight(w_b2t, b2[:, rows].T)
        for pair in range(PAIRS):
            out = dot(w_b2t[...], u1[pair])
            u2_flat[strided(g, 2 * pair), :] = out[:, 0:N3]
            u2_flat[strided(g, 2 * pair + 1), :] = out[:, N3:]

        @pl.when(g == 0)
        def _():
            @pl.when(jnp.logical_or(ka == 0, ka == BLOCKS - 1))
            def _():
                pl.semaphore_wait(barrier, PEERS)

            @pl.when(jnp.logical_and(ka > 0, ka < BLOCKS - 1))
            def _():
                pl.semaphore_wait(barrier, PEERS + 1)

        turn = lax.rem(g, 2)

        def place(s):
            where = line(s // 4)
            pair = lax.rem(pair_of(g) + s, 4)
            away = lax.rem(my_z - turn - 2 * pair + 2 * PLANES, PLANES)
            upper = jnp.logical_and(away >= 1, away <= NEAR).astype(jnp.int32)
            plane = lax.rem(2 * pair + upper + turn, PLANES)
            return g * SPAN + (where * 4 + pair) * OWN, where * PLANES + plane

        def send(s):
            column, p = place(s)
            pltpu.make_async_remote_copy(
                u2.at[pl.ds(column, OWN)],
                cols.at[g, :, my_line, my_z],
                fwd_send.at[g],
                fwd_recv.at[g],
                device_id=(p, ka),
                device_id_type=MESH,
            ).start()

        loop(1, SERVED, send)
        pltpu.make_async_copy(
            u2.at[pl.ds(place(0)[0], OWN)], cols.at[g, :, my_line, my_z], fwd_recv.at[g]
        ).start()

    def hand_over(g):
        pltpu.make_async_copy(cols.at[g, 0:HALVES], cols.at[g, 0:HALVES], fwd_recv.at[g]).wait()
        partner = lax.rem(my_z + 1 - 2 * side(g) + PLANES, PLANES)
        for n in range(NEAR):
            part = cols.at[g, :, :, near_plane(g, n)]
            pltpu.make_async_remote_copy(
                part,
                part,
                hand_send.at[g],
                hand_recv.at[g],
                device_id=(my_line * PLANES + partner, ka),
                device_id_type=MESH,
            ).start()

    def give(g, buffer, target, send_sem, recv_sem):
        home = pl.ds(g * SPAN + (my_line * 4 + pair_of(g)) * OWN, OWN)

        def send(s):
            where, n = line(s // NEAR), lax.rem(s, NEAR)
            pltpu.make_async_remote_copy(
                buffer.at[g, :, n, where],
                target.at[home],
                send_sem.at[g],
                recv_sem.at[g],
                device_id=(where * PLANES + near_plane(g, n), ka),
                device_id_type=MESH,
            ).start()

        loop(1, SERVED, send)
        pltpu.make_async_copy(
            buffer.at[g, :, 0, my_line], target.at[home], recv_sem.at[g]
        ).start()

    def in_columns(g):
        pltpu.make_async_copy(cols.at[g, 0:HALVES], cols.at[g, 0:HALVES], hand_recv.at[g]).wait()

        @pl.loop(0, HALVES)
        def _(half):
            for t in range(2):
                high, low = split(cols[g, 2 * half + t].reshape(N1, N3))
                lx[0:N1, 0:N3] = high
                lx[0:N1, N3:] = low
                both = dot(lx[0:N1, :], w_c[...])
                put_data(data, both[:, 0:N3] + both[:, N3:], t * N3)
            coeff = dot(w_b1t[...], data[...])
            for t in range(2):
                column = g * SPAN + (my_line * 4 + pair_of(g)) * OWN + 2 * half + t
                level = (
                    lev1[...] + levels_second[column] + levels_third[...] - shift_energy
                )
                filt = level / (level * level + damping * damping)
                put_data(data, coeff[:, t * N3 : (t + 1) * N3] * filt, t * N3)
            out = dot(w_xy[lax.rem(g, 2)], data[...])
            for t in range(2):
                part = out[:, t * N3 : (t + 1) * N3].reshape(2, NEAR, LINES, ROWS, N3)
                xs[g, 2 * half + t] = part[0]
                ys[g, 2 * half + t] = part[1]

        give(g, xs, xr, x_send, x_recv)

    def give_bent(g):
        give(g, ys, yr, y_send, y_recv)

    def in_slab(g):
        rows = pl.ds(pl.multiple_of(g * SPAN, SPAN), SPAN)
        pltpu.make_async_copy(xr.at[rows], xr.at[rows], x_recv.at[g]).wait()

        @pl.when(ka > 0)
        def _():
            pltpu.make_async_remote_copy(
                xr.at[rows],
                above.at[rows],
                up_send.at[g],
                up_recv.at[g],
                device_id=(me, ka - 1),
                device_id_type=MESH,
            ).start()

        @pl.when(ka < BLOCKS - 1)
        def _():
            pltpu.make_async_remote_copy(
                xr.at[rows],
                below.at[rows],
                down_send.at[g],
                down_recv.at[g],
                device_id=(me, ka + 1),
                device_id_type=MESH,
            ).start()

        @pl.when(g > 0)
        def _():
            give_bent(g - 1)

        @pl.when(g == GROUPS - 1)
        def _():
            give_bent(g)

        for i in range(ROWS):
            high, low = split(xr_flat[strided(g, i), :])
            lx[i * SPAN : (i + 1) * SPAN, 0:N3] = high
            lx[i * SPAN : (i + 1) * SPAN, N3:] = low

        @pl.loop(0, PAIRS)
        def _(pair):
            for t in range(2):
                at = pl.ds(pl.multiple_of((2 * pair + t) * SPAN, SPAN), SPAN)
                here = dot(lx[at, :], w_a[...]) + dot(lx[at, 0:N3], w_al[...])
                put_data(t1.at[pair], here[:, 0:N3], t * N3, lax.rem(g, 2) * 3 * SPAN)
                angular[2 * pair + t, rows, :] = here[:, N3:]

        @pl.when(lax.rem(g, 2) == 1)
        def _():
            both = pl.ds(pl.multiple_of(g // 2 * 6 * SPAN, 6 * SPAN), 6 * SPAN)

            @pl.loop(0, PAIRS)
            def _(pair):
                out = dot(w_b2[:, both], t1[pair])
                for t in range(2):
                    pot[2 * pair + t] += out[:, t * N3 : (t + 1) * N3]
                out = dot(w_kb[:, both], t1[pair])
                for t in range(2):
                    src[2 * pair + t] -= out[:, t * N3 : (t + 1) * N3]

    def between_blocks(g, last=False):
        rows = pl.ds(pl.multiple_of(g * SPAN, SPAN), SPAN)

        @pl.when(ka < BLOCKS - 1)
        def _():
            pltpu.make_async_copy(above.at[rows], above.at[rows], up_recv.at[g]).wait()

        @pl.when(ka > 0)
        def _():
            pltpu.make_async_copy(below.at[rows], below.at[rows], down_recv.at[g]).wait()

        for i in range(ROWS):
            at = slice(i * SPAN, (i + 1) * SPAN)
            high, low = split(above_flat[strided(g, i), :])
            lx[at, 0:N3] = high
            ly[at, 0:N3] = low
            high, low = split(below_flat[strided(g, i), :])
            lx[at, N3:] = high
            ly[at, N3:] = low

        @pl.loop(0, PAIRS)
        def _(pair):
            for t in range(2):
                at = pl.ds(pl.multiple_of((2 * pair + t) * SPAN, SPAN), SPAN)
                mixed = dot(lx[at, :], w_v[...])
                mixed = mixed[:, 0:N3] + mixed[:, N3:] + dot(ly[at, :], w_vl[...])
                put_data(tv.at[pair], mixed, t * N3, lax.rem(g, 2) * 3 * SPAN)

        @pl.when(lax.rem(g, 2) == 1)
        def _():
            both = pl.ds(pl.multiple_of(g // 2 * 6 * SPAN, 6 * SPAN), 6 * SPAN)

            @pl.loop(0, PAIRS)
            def _(pair):
                out = dot(w_b2[:, both], tv[pair])
                for t in range(2):
                    acc_v[2 * pair + t] += out[:, t * N3 : (t + 1) * N3]
                if last:
                    two = pl.ds(2 * pair, 2)
                    src[two] -= wide[two] * acc_v[two]
                    pltpu.make_async_copy(
                        src.at[two], residual_out.at[0, two], out_sem.at[1]
                    ).start()

    way_out(0)

    @pl.loop(0, 2 * GROUPS - 1)
    def _(step):
        @pl.when(step == 0)
        def _():
            way_out(1)

            loads[2].wait()
            high, low = split(b3[...])
            w_c[0:N3, 0:N3] = high
            w_c[N3:, 0:N3] = high
            w_c[0:N3, N3:] = low
            w_c[N3:, N3:] = jnp.zeros((N3, N3), bf16)
            loads[3].wait()

            @pl.loop(0, N1 // N3)
            def _(n):
                at = pl.multiple_of(n * N3, N3)
                put_weight(w_b1t, b1[:, pl.ds(at, N3)].T, at)

            for n in range(N1 // N3):
                lev1[n * N3 : (n + 1) * N3, :] = spread(levels_first[n : n + 1, :])


        @pl.when(step < GROUPS)
        def _():
            hand_over(step)

        @pl.when(step < GROUPS - 2)
        def _():
            way_out(step + 2)

        @pl.when(step == 0)
        def _():
            loads[4].wait()

            for turn in range(2):

                def gather(s, turn=turn):
                    start = pl.multiple_of(
                        lax.rem(s, LINES) * PLANES * ROWS + near_plane(turn, s // LINES) * ROWS, ROWS
                    )
                    to = pl.multiple_of(s * ROWS, ROWS)
                    picked[pl.ds(to, ROWS), :] = b1[pl.ds(start, ROWS), :]
                    picked[pl.ds(N1 // 2 + to, ROWS), :] = k1[pl.ds(start, ROWS), :]

                loop(0, SERVED, gather)

                @pl.loop(0, 2)
                def _(half, turn=turn):
                    at = pl.multiple_of(half * N3, N3)
                    put_weight(w_xy.at[turn], picked[pl.ds(at, N3), :], at)
                    put_weight(w_tmp, picked[pl.ds(N1 // 2 + at, N3), :], at)

                @pl.loop(0, 2)
                def _(half):
                    at = pl.ds(pl.multiple_of(half * 256, 256), 256)
                    put_data(data, b1[:, at], 0)
                    picked[N1 // 2 :, at] = dot(w_tmp[0 : N1 // 2, :], data[...])

                @pl.loop(0, 2)
                def _(half, turn=turn):
                    at = pl.multiple_of(N1 // 2 + half * N3, N3)
                    put_weight(w_xy.at[turn], picked[pl.ds(at, N3), :], at)


        @pl.when(step == 1)
        def _():
            loads[5].wait()
            loads[6].wait()
            kval = ka.astype(f32)
            reach = [math.sqrt((BLOCKS - 1) * BLOCKS - k * (k + 1)) for k in range(BLOCKS)]

            def by_block(values):
                out = f32(values[-1])
                for k in range(BLOCKS - 1):
                    out = jnp.where(ka == k, f32(values[k]), out)
                return out

            coupled_up = by_block(reach)
            coupled_down = by_block([0.0] + reach[:-1])
            turned = b3[...].T
            exact = functools.partial(
                jnp.dot, preferred_element_type=f32, precision=lax.Precision.HIGHEST
            )
            high, low = split(turned)
            high_k, low_k = split(exact(turned, k3[...].T))
            w_a[0:N3, 0:N3] = high
            w_a[N3:, 0:N3] = high
            w_a[0:N3, N3:] = high_k
            w_a[N3:, N3:] = high_k
            w_al[:, 0:N3] = low
            w_al[:, N3:] = low_k
            w_b[0:N3, 0:N3] = high
            w_b[N3:, 0:N3] = high
            w_b[0:N3, N3:] = low
            w_b[N3:, N3:] = jnp.zeros((N3, N3), bf16)
            high, low = split(exact(turned, cor[...].T) * coupled_up)
            w_v[0:N3, 0:N3] = high
            w_v[0:N3, N3:] = low
            w_vl[0:N3, :] = high
            high, low = split(exact(turned, cor[...]) * coupled_down)
            w_v[N3:, 0:N3] = high
            w_v[N3:, N3:] = low
            w_vl[N3:, :] = high

            @pl.loop(0, GROUPS)
            def _(g):
                part = b2[:, pl.ds(pl.multiple_of(g * SPAN, SPAN), SPAN)]
                put_weight(w_b2, part, 0, g * 3 * SPAN)

            loads[7].wait()

            @pl.loop(0, N2 // N3)
            def _(n):
                at = pl.multiple_of(n * N3, N3)
                put_weight(w_tmp, k2[pl.ds(at, N3), :], at)

            @pl.loop(0, 2)
            def _(half):
                put_data(data, b2[:, pl.ds(pl.multiple_of(half * 256, 256), 256)], 0)
                out = dot(w_tmp[...], data[...])
                for n in range(256 // SPAN):
                    part = out[:, n * SPAN : (n + 1) * SPAN]
                    put_weight(w_kb, part, 0, (half * (256 // SPAN) + n) * 3 * SPAN)

            loads[8].wait()
            loads[9].wait()

            @pl.loop(0, N2 // N3)
            def _(n):
                at = pl.ds(pl.multiple_of(n * N3, N3), N3)
                factors = rot[:, at]
                for i in range(ROWS):
                    factor = spread(factors[i : i + 1, :])
                    wide[i, at, :] = factor
                    diag[i, at, :] = pot[i, at, :] + kval * kval * factor - shift_energy
                    pot[i, at, :] = jnp.zeros((N3, N3), f32)
                    acc_v[i, at, :] = jnp.zeros((N3, N3), f32)

            @pl.when(ka == 0)
            def _():
                below[...] = jnp.zeros(below.shape, f32)

            @pl.when(ka == BLOCKS - 1)
            def _():
                above[...] = jnp.zeros(above.shape, f32)


        @pl.when(jnp.logical_and(step >= 1, step <= GROUPS))
        def _():
            in_columns(step - 1)

        @pl.when(step >= GROUPS - 1)
        def _():
            in_slab(step - GROUPS + 1)

        @pl.when(step > GROUPS)
        def _():
            between_blocks(step - GROUPS - 1)

    results = [pltpu.make_async_copy(pot, solved_out.at[0], out_sem.at[0])]
    results[0].start()
    between_blocks(GROUPS - 2)

    @pl.loop(0, ROWS)
    def _(i):
        src[i] -= diag[i] * pot[i]

    @pl.loop(0, GROUPS)
    def _(g):
        rows = pl.ds(pl.multiple_of(g * SPAN, SPAN), SPAN)
        pltpu.make_async_copy(yr.at[rows], yr.at[rows], y_recv.at[g]).wait()
        for i in range(ROWS):
            high, low = split(yr_flat[strided(g, i), :])
            ly[i * SPAN : (i + 1) * SPAN, 0:N3] = high
            ly[i * SPAN : (i + 1) * SPAN, N3:] = low

        @pl.loop(0, PAIRS)
        def _(pair):
            for t in range(2):
                at = pl.ds(pl.multiple_of((2 * pair + t) * SPAN, SPAN), SPAN)
                bent = dot(ly[at, :], w_b[...])
                bent = bent[:, 0:N3] + bent[:, N3:] + angular[2 * pair + t, rows, :]
                put_data(t2.at[pair], bent, t * N3)
            each = pl.ds(pl.multiple_of(g * 3 * SPAN, 3 * SPAN), 3 * SPAN)
            out = dot(w_b2[:, each], t2[pair])
            for t in range(2):
                src[2 * pair + t] -= out[:, t * N3 : (t + 1) * N3]

    between_blocks(GROUPS - 1, last=True)
    results.append(pltpu.make_async_copy(src, residual_out.at[0], out_sem.at[1]))

    @pl.loop(0, GROUPS)
    def _(g):
        rows = pl.ds(g * SPAN, SPAN)
        part = u2.at[pl.ds(0, (SERVED - 1) * OWN)]
        pltpu.make_async_copy(part, part, fwd_send.at[g]).wait()
        pltpu.make_async_copy(part, part, x_send.at[g]).wait()
        pltpu.make_async_copy(part, part, y_send.at[g]).wait()
        pltpu.make_async_copy(cols.at[g, 0:HALVES], cols.at[g, 0:HALVES], hand_send.at[g]).wait()

        @pl.when(ka > 0)
        def _():
            pltpu.make_async_copy(xr.at[rows], xr.at[rows], up_send.at[g]).wait()

        @pl.when(ka < BLOCKS - 1)
        def _():
            pltpu.make_async_copy(xr.at[rows], xr.at[rows], down_send.at[g]).wait()

    for copy in results:
        copy.wait()


def hand_out(solved, residual, solved_out, residual_out, held, in_sem, out_sem):
    pieces = 4
    ways = ((solved, solved_out), (residual, residual_out))
    rows = [pl.ds(n * ROWS // pieces, ROWS // pieces) for n in range(pieces)]

    def copies(way, n, inward):
        source, target = ways[way]
        here = held.at[way, rows[n]]
        if inward:
            return pltpu.make_async_copy(source.at[0, rows[n]], here, in_sem.at[way, n])
        return pltpu.make_async_copy(here, target.at[0, rows[n]], out_sem.at[way, n])

    order = [(way, n) for way in range(2) for n in range(pieces)]
    for way, n in order:
        copies(way, n, True).start()
    for way, n in order:
        copies(way, n, True).wait()
        copies(way, n, False).start()
    for way, n in order:
        copies(way, n, False).wait()


def per_device(
    states,
    potential,
    rotation_factor,
    basis_first,
    basis_second,
    basis_third,
    levels_first,
    levels_second,
    levels_third,
    kinetic_first,
    kinetic_second,
    kinetic_third,
    coriolis_matrix,
):
    vmem, dma = pltpu.VMEM, pltpu.SemaphoreType.DMA
    anywhere = pl.BlockSpec(memory_space=pl.ANY)
    here = pl.BlockSpec(memory_space=pltpu.VMEM)
    slab = (ROWS, N2, N3)
    turned = (N2, ROWS, N3)
    columns = (GROUPS, OWN, LINES, PLANES, ROWS, N3)
    given = (GROUPS, OWN, NEAR, LINES, ROWS, N3)
    weight = vmem((N1, 3 * N1), bf16)
    parts = vmem((N2, GROUPS * 3 * SPAN), bf16)
    stacked = vmem((PAIRS, 6 * SPAN, 2 * N3), bf16)
    square = vmem((N1, N1), f32)
    small = vmem((N3, N3), f32)
    scratch = [
        vmem(slab, f32),
        vmem(slab, f32),
        vmem((ROWS, N2), f32),
        square,
        square,
        square,
        square,
        small,
        small,
        small,
        vmem((SPAN, 3 * N2), bf16),
        weight,
        weight,
        vmem((2, N1, 3 * N1), bf16),
        parts,
        parts,
        vmem((PAIRS, 3 * N2, 2 * N3), bf16),
        vmem(turned, f32),
        vmem(columns, f32),
        vmem(given, f32),
        vmem(given, f32),
        vmem(turned, f32),
        vmem(turned, f32),
        vmem(turned, f32),
        vmem(turned, f32),
        vmem((3 * N1, 2 * N3), bf16),
        vmem((ROWS * SPAN, 2 * N3), bf16),
        vmem((ROWS * SPAN, 2 * N3), bf16),
        stacked,
        vmem((PAIRS, 3 * SPAN, 2 * N3), bf16),
        stacked,
        vmem(slab, f32),
        vmem((2 * N3, 2 * N3), bf16),
        vmem((2 * N3, 2 * N3), bf16),
        vmem((N3, 2 * N3), bf16),
        vmem((2 * N3, 2 * N3), bf16),
        vmem((2 * N3, 2 * N3), bf16),
        vmem((2 * N3, N3), bf16),
        vmem(slab, f32),
        vmem(slab, f32),
        vmem(slab, f32),
        vmem((N1, N3), f32),
        square,
        dma((10,)),
        dma((2,)),
    ] + [dma((GROUPS,))] * 12
    shapes = (jax.ShapeDtypeStruct((1,) + slab, f32),) * 2
    solved, residual = pl.pallas_call(
        kernel,
        out_shape=shapes,
        in_specs=[anywhere] * 6
        + [here, pl.BlockSpec(memory_space=pltpu.SMEM), here]
        + [anywhere] * 4,
        out_specs=(anywhere, anywhere),
        scratch_shapes=scratch,
        compiler_params=pltpu.CompilerParams(
            collective_id=0, has_side_effects=True, vmem_limit_bytes=66_000_000
        ),
        name="filter_step",
    )(
        states,
        potential,
        rotation_factor,
        basis_first,
        basis_second,
        basis_third,
        levels_first.reshape(N1 // N3, N3),
        levels_second,
        levels_third.reshape(1, N3),
        kinetic_first,
        kinetic_second,
        kinetic_third,
        coriolis_matrix,
    )
    return pl.pallas_call(
        hand_out,
        out_shape=shapes,
        in_specs=[anywhere] * 2,
        out_specs=(anywhere,) * 2,
        scratch_shapes=[vmem((2,) + slab, f32), dma((2, 4)), dma((2, 4))],
        name="tail",
    )(solved, residual)


def solution(mesh):
    return jax.shard_map(
        per_device,
        mesh=mesh,
        in_specs=(
            P("ka", "coord", None, None),
            P("coord", None, None),
            P("coord", None),
            P(),
            P(),
            P(),
            P(),
            P(),
            P(),
            P(),
            P(),
            P(),
            P(),
        ),
        out_specs=(P("ka", "coord", None, None), P("ka", "coord", None, None)),
        check_vma=False,
    )
```

```python
import functools
import math

import jax
import jax.numpy as jnp
from jax import lax
from jax.experimental import pallas as pl
from jax.experimental.pallas import tpu as pltpu
from jax.sharding import PartitionSpec as P

MESH = pl.DeviceIdType.MESH
f32 = jnp.float32
bf16 = jnp.bfloat16
shift_energy = 2.5
damping = 0.5

PEERS = 64
BLOCKS = 4
GROUPS = 4
N1 = 512
N2 = 512
N3 = 128
ROWS = N1 // PEERS
PAIRS = ROWS // 2
SPAN = N2 // GROUPS
OWN = 4
HALVES = OWN // 2
PLANES = 8
NEAR = 4
LINES = PEERS // PLANES
SERVED = NEAR * LINES


def split(value):
    high = value.astype(bf16)
    return high, (value - high.astype(f32)).astype(bf16)


def dot(left, right):
    return jnp.dot(left, right, preferred_element_type=f32)


def put_weight(ref, value, offset=0, base=0):
    high, low = split(value)
    width = value.shape[1]
    for place, part in enumerate((high, low, high)):
        lanes = pl.ds(pl.multiple_of(base + place * width, N3), width)
        ref[pl.ds(offset, value.shape[0]), lanes] = part


def put_data(ref, value, lane, base=0):
    high, low = split(value)
    height, width = value.shape
    for place, part in enumerate((high, high, low)):
        rows = pl.ds(pl.multiple_of(base + place * height, N3), height)
        ref[rows, pl.ds(lane, width)] = part


def spread(row, height=N3):
    return jnp.broadcast_to(row, (height, row.shape[1])).T


def kernel(
    states,
    potential,
    rotation,
    first,
    second,
    third,
    levels_first,
    levels_second,
    levels_third,
    kin_first,
    kin_second,
    kin_third,
    coriolis,
    solved_out,
    residual_out,
    src,
    pot,
    rot,
    b1,
    b2,
    k1,
    k2,
    b3,
    k3,
    cor,
    w_b2t,
    w_b1t,
    w_tmp,
    w_xy,
    w_b2,
    w_kb,
    u1,
    u2,
    cols,
    xs,
    ys,
    xr,
    yr,
    above,
    below,
    data,
    lx,
    ly,
    t1,
    t2,
    tv,
    angular,
    w_c,
    w_a,
    w_al,
    w_b,
    w_v,
    w_vl,
    acc_v,
    diag,
    wide,
    lev1,
    picked,
    load_sem,
    out_sem,
    fwd_send,
    fwd_recv,
    hand_send,
    hand_recv,
    x_send,
    x_recv,
    y_send,
    y_recv,
    up_send,
    up_recv,
    down_send,
    down_recv,
):
    me = lax.axis_index("coord")
    ka = lax.axis_index("ka")
    my_y, my_x, my_z = me // 16, lax.rem(me // 8, 2), lax.rem(me, 8)
    my_line = me // PLANES

    def side(g):
        return lax.rem(my_z + lax.rem(g, 2), 2)

    def pair_of(g):
        return lax.rem(my_z - lax.rem(g, 2) + PLANES, PLANES) // 2

    def near_plane(g, n):
        return lax.rem(my_z + (2 * side(g) - 1) * n + PLANES, PLANES)

    def line(step):
        return lax.rem(my_y + step // 2, 4) * 2 + lax.rem(my_x + step, 2)

    def loop(start, stop, body):
        def step(s, carry):
            body(s)
            return carry

        lax.fori_loop(start, stop, step, 0)

    loads = [
        pltpu.make_async_copy(source, target, load_sem.at[index])
        for index, (source, target) in enumerate(
            (
                (second, b2),
                (states.at[0], src),
                (third, b3),
                (first, b1),
                (kin_first, k1),
                (kin_third, k3),
                (coriolis, cor),
                (kin_second, k2),
                (potential, pot),
                (rotation, rot),
            )
        )
    ]
    for copy in loads[:2]:
        copy.start()
    barrier = pltpu.get_barrier_semaphore()
    def greet(s):
        p = line(s // PLANES) * PLANES + lax.rem(my_z + s, PLANES)
        pl.semaphore_signal(barrier, inc=1, device_id=(p, ka), device_id_type=MESH)

    loop(1, PEERS, greet)

    @pl.when(ka > 0)
    def _():
        pl.semaphore_signal(barrier, inc=1, device_id=(me, ka - 1), device_id_type=MESH)

    @pl.when(ka < BLOCKS - 1)
    def _():
        pl.semaphore_signal(barrier, inc=1, device_id=(me, ka + 1), device_id_type=MESH)

    loads[0].wait()

    loads[1].wait()
    for copy in loads[2:]:
        copy.start()

    @pl.loop(0, PAIRS)
    def _(pair):
        for t in range(2):
            put_data(u1.at[pair], src[2 * pair + t], t * N3)

    def strided(g, i):
        return pl.ds(g * SPAN * ROWS + i, SPAN, stride=ROWS)

    flat = (N2 * ROWS, N3)
    u2_flat, xr_flat, yr_flat = u2.reshape(flat), xr.reshape(flat), yr.reshape(flat)
    above_flat, below_flat = above.reshape(flat), below.reshape(flat)

    def way_out(g):
        rows = pl.ds(pl.multiple_of(g * SPAN, SPAN), SPAN)
        put_weight(w_b2t, b2[:, rows].T)
        for pair in range(PAIRS):
            out = dot(w_b2t[...], u1[pair])
            u2_flat[strided(g, 2 * pair), :] = out[:, 0:N3]
            u2_flat[strided(g, 2 * pair + 1), :] = out[:, N3:]

        @pl.when(g == 0)
        def _():
            @pl.when(jnp.logical_or(ka == 0, ka == BLOCKS - 1))
            def _():
                pl.semaphore_wait(barrier, PEERS)

            @pl.when(jnp.logical_and(ka > 0, ka < BLOCKS - 1))
            def _():
                pl.semaphore_wait(barrier, PEERS + 1)

        turn = lax.rem(g, 2)

        def place(s):
            where = line(s // 4)
            pair = lax.rem(pair_of(g) + s, 4)
            away = lax.rem(my_z - turn - 2 * pair + 2 * PLANES, PLANES)
            upper = jnp.logical_and(away >= 1, away <= NEAR).astype(jnp.int32)
            plane = lax.rem(2 * pair + upper + turn, PLANES)
            return g * SPAN + (where * 4 + pair) * OWN, where * PLANES + plane

        def send(s):
            column, p = place(s)
            pltpu.make_async_remote_copy(
                u2.at[pl.ds(column, OWN)],
                cols.at[g, :, my_line, my_z],
                fwd_send.at[g],
                fwd_recv.at[g],
                device_id=(p, ka),
                device_id_type=MESH,
            ).start()

        loop(1, SERVED, send)
        pltpu.make_async_copy(
            u2.at[pl.ds(place(0)[0], OWN)], cols.at[g, :, my_line, my_z], fwd_recv.at[g]
        ).start()

    def hand_over(g):
        pltpu.make_async_copy(cols.at[g, 0:HALVES], cols.at[g, 0:HALVES], fwd_recv.at[g]).wait()
        partner = lax.rem(my_z + 1 - 2 * side(g) + PLANES, PLANES)
        for n in range(NEAR):
            part = cols.at[g, :, :, near_plane(g, n)]
            pltpu.make_async_remote_copy(
                part,
                part,
                hand_send.at[g],
                hand_recv.at[g],
                device_id=(my_line * PLANES + partner, ka),
                device_id_type=MESH,
            ).start()

    def give(g, buffer, target, send_sem, recv_sem):
        home = pl.ds(g * SPAN + (my_line * 4 + pair_of(g)) * OWN, OWN)

        def send(s):
            where, n = line(s // NEAR), lax.rem(s, NEAR)
            pltpu.make_async_remote_copy(
                buffer.at[g, :, n, where],
                target.at[home],
                send_sem.at[g],
                recv_sem.at[g],
                device_id=(where * PLANES + near_plane(g, n), ka),
                device_id_type=MESH,
            ).start()

        loop(1, SERVED, send)
        pltpu.make_async_copy(
            buffer.at[g, :, 0, my_line], target.at[home], recv_sem.at[g]
        ).start()

    def in_columns(g):
        pltpu.make_async_copy(cols.at[g, 0:HALVES], cols.at[g, 0:HALVES], hand_recv.at[g]).wait()

        @pl.loop(0, HALVES)
        def _(half):
            for t in range(2):
                high, low = split(cols[g, 2 * half + t].reshape(N1, N3))
                lx[0:N1, 0:N3] = high
                lx[0:N1, N3:] = low
                both = dot(lx[0:N1, :], w_c[...])
                put_data(data, both[:, 0:N3] + both[:, N3:], t * N3)
            coeff = dot(w_b1t[...], data[...])
            for t in range(2):
                column = g * SPAN + (my_line * 4 + pair_of(g)) * OWN + 2 * half + t
                level = (
                    lev1[...] + levels_second[column] + levels_third[...] - shift_energy
                )
                filt = level / (level * level + damping * damping)
                put_data(data, coeff[:, t * N3 : (t + 1) * N3] * filt, t * N3)
            out = dot(w_xy[lax.rem(g, 2)], data[...])
            for t in range(2):
                part = out[:, t * N3 : (t + 1) * N3].reshape(2, NEAR, LINES, ROWS, N3)
                xs[g, 2 * half + t] = part[0]
                ys[g, 2 * half + t] = part[1]

        give(g, xs, xr, x_send, x_recv)

    def give_bent(g):
        give(g, ys, yr, y_send, y_recv)

    def in_slab(g):
        rows = pl.ds(pl.multiple_of(g * SPAN, SPAN), SPAN)
        pltpu.make_async_copy(xr.at[rows], xr.at[rows], x_recv.at[g]).wait()

        @pl.when(ka > 0)
        def _():
            pltpu.make_async_remote_copy(
                xr.at[rows],
                above.at[rows],
                up_send.at[g],
                up_recv.at[g],
                device_id=(me, ka - 1),
                device_id_type=MESH,
            ).start()

        @pl.when(ka < BLOCKS - 1)
        def _():
            pltpu.make_async_remote_copy(
                xr.at[rows],
                below.at[rows],
                down_send.at[g],
                down_recv.at[g],
                device_id=(me, ka + 1),
                device_id_type=MESH,
            ).start()

        give_bent(g)

        for i in range(ROWS):
            high, low = split(xr_flat[strided(g, i), :])
            lx[i * SPAN : (i + 1) * SPAN, 0:N3] = high
            lx[i * SPAN : (i + 1) * SPAN, N3:] = low

        @pl.loop(0, PAIRS)
        def _(pair):
            for t in range(2):
                at = pl.ds(pl.multiple_of((2 * pair + t) * SPAN, SPAN), SPAN)
                here = dot(lx[at, :], w_a[...]) + dot(lx[at, 0:N3], w_al[...])
                put_data(t1.at[pair], here[:, 0:N3], t * N3, lax.rem(g, 2) * 3 * SPAN)
                angular[2 * pair + t, rows, :] = here[:, N3:]

        @pl.when(lax.rem(g, 2) == 1)
        def _():
            both = pl.ds(pl.multiple_of(g // 2 * 6 * SPAN, 6 * SPAN), 6 * SPAN)

            @pl.loop(0, PAIRS)
            def _(pair):
                out = dot(w_b2[:, both], t1[pair])
                for t in range(2):
                    pot[2 * pair + t] += out[:, t * N3 : (t + 1) * N3]
                out = dot(w_kb[:, both], t1[pair])
                for t in range(2):
                    src[2 * pair + t] -= out[:, t * N3 : (t + 1) * N3]

    def between_blocks(g):
        rows = pl.ds(pl.multiple_of(g * SPAN, SPAN), SPAN)

        @pl.when(ka < BLOCKS - 1)
        def _():
            pltpu.make_async_copy(above.at[rows], above.at[rows], up_recv.at[g]).wait()

        @pl.when(ka > 0)
        def _():
            pltpu.make_async_copy(below.at[rows], below.at[rows], down_recv.at[g]).wait()

        for i in range(ROWS):
            at = slice(i * SPAN, (i + 1) * SPAN)
            high, low = split(above_flat[strided(g, i), :])
            lx[at, 0:N3] = high
            ly[at, 0:N3] = low
            high, low = split(below_flat[strided(g, i), :])
            lx[at, N3:] = high
            ly[at, N3:] = low

        @pl.loop(0, PAIRS)
        def _(pair):
            for t in range(2):
                at = pl.ds(pl.multiple_of((2 * pair + t) * SPAN, SPAN), SPAN)
                mixed = dot(lx[at, :], w_v[...])
                mixed = mixed[:, 0:N3] + mixed[:, N3:] + dot(ly[at, :], w_vl[...])
                put_data(tv.at[pair], mixed, t * N3, lax.rem(g, 2) * 3 * SPAN)

        @pl.when(lax.rem(g, 2) == 1)
        def _():
            both = pl.ds(pl.multiple_of(g // 2 * 6 * SPAN, 6 * SPAN), 6 * SPAN)

            @pl.loop(0, PAIRS)
            def _(pair):
                out = dot(w_b2[:, both], tv[pair])
                for t in range(2):
                    acc_v[2 * pair + t] += out[:, t * N3 : (t + 1) * N3]

    way_out(0)

    @pl.loop(0, 2 * GROUPS - 1)
    def _(step):
        @pl.when(step == 0)
        def _():
            way_out(1)

            loads[2].wait()
            high, low = split(b3[...])
            w_c[0:N3, 0:N3] = high
            w_c[N3:, 0:N3] = high
            w_c[0:N3, N3:] = low
            w_c[N3:, N3:] = jnp.zeros((N3, N3), bf16)
            loads[3].wait()

            @pl.loop(0, N1 // N3)
            def _(n):
                at = pl.multiple_of(n * N3, N3)
                put_weight(w_b1t, b1[:, pl.ds(at, N3)].T, at)

            for n in range(N1 // N3):
                lev1[n * N3 : (n + 1) * N3, :] = spread(levels_first[n : n + 1, :])


        @pl.when(step < GROUPS)
        def _():
            hand_over(step)

        @pl.when(step < GROUPS - 2)
        def _():
            way_out(step + 2)

        @pl.when(step == 0)
        def _():
            loads[4].wait()

            for turn in range(2):

                def gather(s, turn=turn):
                    start = pl.multiple_of(
                        lax.rem(s, LINES) * PLANES * ROWS + near_plane(turn, s // LINES) * ROWS, ROWS
                    )
                    to = pl.multiple_of(s * ROWS, ROWS)
                    picked[pl.ds(to, ROWS), :] = b1[pl.ds(start, ROWS), :]
                    picked[pl.ds(N1 // 2 + to, ROWS), :] = k1[pl.ds(start, ROWS), :]

                loop(0, SERVED, gather)

                @pl.loop(0, 2)
                def _(half, turn=turn):
                    at = pl.multiple_of(half * N3, N3)
                    put_weight(w_xy.at[turn], picked[pl.ds(at, N3), :], at)
                    put_weight(w_tmp, picked[pl.ds(N1 // 2 + at, N3), :], at)

                @pl.loop(0, 2)
                def _(half):
                    at = pl.ds(pl.multiple_of(half * 256, 256), 256)
                    put_data(data, b1[:, at], 0)
                    picked[N1 // 2 :, at] = dot(w_tmp[0 : N1 // 2, :], data[...])

                @pl.loop(0, 2)
                def _(half, turn=turn):
                    at = pl.multiple_of(N1 // 2 + half * N3, N3)
                    put_weight(w_xy.at[turn], picked[pl.ds(at, N3), :], at)


        @pl.when(step == 1)
        def _():
            loads[5].wait()
            loads[6].wait()
            kval = ka.astype(f32)
            reach = [math.sqrt((BLOCKS - 1) * BLOCKS - k * (k + 1)) for k in range(BLOCKS)]

            def by_block(values):
                out = f32(values[-1])
                for k in range(BLOCKS - 1):
                    out = jnp.where(ka == k, f32(values[k]), out)
                return out

            coupled_up = by_block(reach)
            coupled_down = by_block([0.0] + reach[:-1])
            turned = b3[...].T
            exact = functools.partial(
                jnp.dot, preferred_element_type=f32, precision=lax.Precision.HIGHEST
            )
            high, low = split(turned)
            high_k, low_k = split(exact(turned, k3[...].T))
            w_a[0:N3, 0:N3] = high
            w_a[N3:, 0:N3] = high
            w_a[0:N3, N3:] = high_k
            w_a[N3:, N3:] = high_k
            w_al[:, 0:N3] = low
            w_al[:, N3:] = low_k
            w_b[0:N3, 0:N3] = high
            w_b[N3:, 0:N3] = high
            w_b[0:N3, N3:] = low
            w_b[N3:, N3:] = jnp.zeros((N3, N3), bf16)
            high, low = split(exact(turned, cor[...].T) * coupled_up)
            w_v[0:N3, 0:N3] = high
            w_v[0:N3, N3:] = low
            w_vl[0:N3, :] = high
            high, low = split(exact(turned, cor[...]) * coupled_down)
            w_v[N3:, 0:N3] = high
            w_v[N3:, N3:] = low
            w_vl[N3:, :] = high

            @pl.loop(0, GROUPS)
            def _(g):
                part = b2[:, pl.ds(pl.multiple_of(g * SPAN, SPAN), SPAN)]
                put_weight(w_b2, part, 0, g * 3 * SPAN)

            loads[7].wait()

            @pl.loop(0, N2 // N3)
            def _(n):
                at = pl.multiple_of(n * N3, N3)
                put_weight(w_tmp, k2[pl.ds(at, N3), :], at)

            @pl.loop(0, 2)
            def _(half):
                put_data(data, b2[:, pl.ds(pl.multiple_of(half * 256, 256), 256)], 0)
                out = dot(w_tmp[...], data[...])
                for n in range(256 // SPAN):
                    part = out[:, n * SPAN : (n + 1) * SPAN]
                    put_weight(w_kb, part, 0, (half * (256 // SPAN) + n) * 3 * SPAN)

            loads[8].wait()
            loads[9].wait()

            @pl.loop(0, N2 // N3)
            def _(n):
                at = pl.ds(pl.multiple_of(n * N3, N3), N3)
                factors = rot[:, at]
                for i in range(ROWS):
                    factor = spread(factors[i : i + 1, :])
                    wide[i, at, :] = factor
                    diag[i, at, :] = pot[i, at, :] + kval * kval * factor - shift_energy
                    pot[i, at, :] = jnp.zeros((N3, N3), f32)
                    acc_v[i, at, :] = jnp.zeros((N3, N3), f32)

            @pl.when(ka == 0)
            def _():
                below[...] = jnp.zeros(below.shape, f32)

            @pl.when(ka == BLOCKS - 1)
            def _():
                above[...] = jnp.zeros(above.shape, f32)


        @pl.when(jnp.logical_and(step >= 1, step <= GROUPS))
        def _():
            in_columns(step - 1)

        @pl.when(step >= GROUPS - 1)
        def _():
            in_slab(step - GROUPS + 1)

        @pl.when(step > GROUPS)
        def _():
            between_blocks(step - GROUPS - 1)

    results = [pltpu.make_async_copy(pot, solved_out.at[0], out_sem.at[0])]
    results[0].start()
    between_blocks(GROUPS - 2)

    @pl.loop(0, ROWS)
    def _(i):
        src[i] -= diag[i] * pot[i]

    def bent_in_slab(g, last=False):
        rows = pl.ds(pl.multiple_of(g * SPAN, SPAN), SPAN)
        pltpu.make_async_copy(yr.at[rows], yr.at[rows], y_recv.at[g]).wait()
        for i in range(ROWS):
            high, low = split(yr_flat[strided(g, i), :])
            ly[i * SPAN : (i + 1) * SPAN, 0:N3] = high
            ly[i * SPAN : (i + 1) * SPAN, N3:] = low

        @pl.loop(0, PAIRS)
        def _(pair):
            for t in range(2):
                at = pl.ds(pl.multiple_of((2 * pair + t) * SPAN, SPAN), SPAN)
                bent = dot(ly[at, :], w_b[...])
                bent = bent[:, 0:N3] + bent[:, N3:] + angular[2 * pair + t, rows, :]
                put_data(t2.at[pair], bent, t * N3)
            each = pl.ds(pl.multiple_of(g * 3 * SPAN, 3 * SPAN), 3 * SPAN)
            out = dot(w_b2[:, each], t2[pair])
            for t in range(2):
                src[2 * pair + t] -= out[:, t * N3 : (t + 1) * N3]
            if last:
                two = pl.ds(2 * pair, 2)
                src[two] -= wide[two] * acc_v[two]
                pltpu.make_async_copy(
                    src.at[two], residual_out.at[0, two], out_sem.at[1]
                ).start()

    pl.loop(0, GROUPS - 1)(bent_in_slab)
    between_blocks(GROUPS - 1)
    bent_in_slab(GROUPS - 1, last=True)
    results.append(pltpu.make_async_copy(src, residual_out.at[0], out_sem.at[1]))

    @pl.loop(0, GROUPS)
    def _(g):
        rows = pl.ds(g * SPAN, SPAN)
        part = u2.at[pl.ds(0, (SERVED - 1) * OWN)]
        pltpu.make_async_copy(part, part, fwd_send.at[g]).wait()
        pltpu.make_async_copy(part, part, x_send.at[g]).wait()
        pltpu.make_async_copy(part, part, y_send.at[g]).wait()
        pltpu.make_async_copy(cols.at[g, 0:HALVES], cols.at[g, 0:HALVES], hand_send.at[g]).wait()

        @pl.when(ka > 0)
        def _():
            pltpu.make_async_copy(xr.at[rows], xr.at[rows], up_send.at[g]).wait()

        @pl.when(ka < BLOCKS - 1)
        def _():
            pltpu.make_async_copy(xr.at[rows], xr.at[rows], down_send.at[g]).wait()

    for copy in results:
        copy.wait()


def hand_out(solved, residual, solved_out, residual_out, held, in_sem, out_sem):
    pieces = 8
    ways = ((solved, solved_out), (residual, residual_out))
    rows = [pl.ds(n * ROWS // pieces, ROWS // pieces) for n in range(pieces)]

    def copies(way, n, inward):
        source, target = ways[way]
        here = held.at[way, rows[n]]
        if inward:
            return pltpu.make_async_copy(source.at[0, rows[n]], here, in_sem.at[way, n])
        return pltpu.make_async_copy(here, target.at[0, rows[n]], out_sem.at[way, n])

    order = [(way, n) for way in range(2) for n in range(pieces)]
    for way, n in order:
        copies(way, n, True).start()
    for way, n in order:
        copies(way, n, True).wait()
        copies(way, n, False).start()
    for way, n in order:
        copies(way, n, False).wait()


def per_device(
    states,
    potential,
    rotation_factor,
    basis_first,
    basis_second,
    basis_third,
    levels_first,
    levels_second,
    levels_third,
    kinetic_first,
    kinetic_second,
    kinetic_third,
    coriolis_matrix,
):
    vmem, dma = pltpu.VMEM, pltpu.SemaphoreType.DMA
    anywhere = pl.BlockSpec(memory_space=pl.ANY)
    here = pl.BlockSpec(memory_space=pltpu.VMEM)
    slab = (ROWS, N2, N3)
    turned = (N2, ROWS, N3)
    columns = (GROUPS, OWN, LINES, PLANES, ROWS, N3)
    given = (GROUPS, OWN, NEAR, LINES, ROWS, N3)
    weight = vmem((N1, 3 * N1), bf16)
    parts = vmem((N2, GROUPS * 3 * SPAN), bf16)
    stacked = vmem((PAIRS, 6 * SPAN, 2 * N3), bf16)
    square = vmem((N1, N1), f32)
    small = vmem((N3, N3), f32)
    scratch = [
        vmem(slab, f32),
        vmem(slab, f32),
        vmem((ROWS, N2), f32),
        square,
        square,
        square,
        square,
        small,
        small,
        small,
        vmem((SPAN, 3 * N2), bf16),
        weight,
        weight,
        vmem((2, N1, 3 * N1), bf16),
        parts,
        parts,
        vmem((PAIRS, 3 * N2, 2 * N3), bf16),
        vmem(turned, f32),
        vmem(columns, f32),
        vmem(given, f32),
        vmem(given, f32),
        vmem(turned, f32),
        vmem(turned, f32),
        vmem(turned, f32),
        vmem(turned, f32),
        vmem((3 * N1, 2 * N3), bf16),
        vmem((ROWS * SPAN, 2 * N3), bf16),
        vmem((ROWS * SPAN, 2 * N3), bf16),
        stacked,
        vmem((PAIRS, 3 * SPAN, 2 * N3), bf16),
        stacked,
        vmem(slab, f32),
        vmem((2 * N3, 2 * N3), bf16),
        vmem((2 * N3, 2 * N3), bf16),
        vmem((N3, 2 * N3), bf16),
        vmem((2 * N3, 2 * N3), bf16),
        vmem((2 * N3, 2 * N3), bf16),
        vmem((2 * N3, N3), bf16),
        vmem(slab, f32),
        vmem(slab, f32),
        vmem(slab, f32),
        vmem((N1, N3), f32),
        square,
        dma((10,)),
        dma((2,)),
    ] + [dma((GROUPS,))] * 12
    shapes = (jax.ShapeDtypeStruct((1,) + slab, f32),) * 2
    solved, residual = pl.pallas_call(
        kernel,
        out_shape=shapes,
        in_specs=[anywhere] * 6
        + [here, pl.BlockSpec(memory_space=pltpu.SMEM), here]
        + [anywhere] * 4,
        out_specs=(anywhere, anywhere),
        scratch_shapes=scratch,
        compiler_params=pltpu.CompilerParams(
            collective_id=0, has_side_effects=True, vmem_limit_bytes=66_000_000
        ),
        name="filter_step",
    )(
        states,
        potential,
        rotation_factor,
        basis_first,
        basis_second,
        basis_third,
        levels_first.reshape(N1 // N3, N3),
        levels_second,
        levels_third.reshape(1, N3),
        kinetic_first,
        kinetic_second,
        kinetic_third,
        coriolis_matrix,
    )
    return pl.pallas_call(
        hand_out,
        out_shape=shapes,
        in_specs=[anywhere] * 2,
        out_specs=(anywhere,) * 2,
        scratch_shapes=[vmem((2,) + slab, f32), dma((2, 8)), dma((2, 8))],
        name="tail",
    )(solved, residual)


def solution(mesh):
    return jax.shard_map(
        per_device,
        mesh=mesh,
        in_specs=(
            P("ka", "coord", None, None),
            P("coord", None, None),
            P("coord", None),
            P(),
            P(),
            P(),
            P(),
            P(),
            P(),
            P(),
            P(),
            P(),
            P(),
        ),
        out_specs=(P("ka", "coord", None, None), P("ka", "coord", None, None)),
        check_vma=False,
    )
```
